256 devices in a mesh: dp: 4 (over y_lo, core), wide: 64 (over y_hi, z, x).
Axes of the slice: x: 4, y: 4 (y_hi: 2, y_lo: 2; y = y_hi * 2 + y_lo), z: 8, core: 2. Of those that a mesh axis runs over, the one named last changes fastest.
Arguments:
- layer_in: bfloat16 [1024, 4096], P('wide', 'dp'), may hold values from -6 to 6
- route_ids: int32 [1024, 8], P('wide'), may hold values from 0 to 63, all different within a row; in each aligned block of 16 rows (0 to 15, 16 to 31, ...) at most 4 rows name the same one
- route_scores: float32 [1024, 8], P('wide'), may hold values from 0.05 to 1
- expert_gate: bfloat16 [64, 1536, 4096], P('wide', None, 'dp'), may hold values from -0.09375 to 0.09375
- expert_up: bfloat16 [64, 1536, 4096], P('wide', None, 'dp'), may hold values from -0.09375 to 0.09375
- expert_down: bfloat16 [64, 1536, 4096], P('wide', None, 'dp'), may hold values from -0.15625 to 0.15625
- student_gate: bfloat16 [12288, 4096], P('wide', 'dp'), may hold values from -0.09375 to 0.09375
- student_up: bfloat16 [12288, 4096], P('wide', 'dp'), may hold values from -0.09375 to 0.09375
- student_down: bfloat16 [12288, 4096], P('wide', 'dp'), may hold values from -0.0546875 to 0.0546875
Outputs:
- teacher_out: bfloat16 [1024, 4096], P('wide', 'dp')
- grad_gate: bfloat16 [12288, 4096], P('wide', 'dp')
- grad_up: bfloat16 [12288, 4096], P('wide', 'dp')
- grad_down: bfloat16 [12288, 4096], P('wide', 'dp')
The draws below stay inside these ranges and needn't reach their ends.
Inputs may be any that keep to these rules, and one draw needn't show every extreme that they name: `route_ids`: each row names 8 different experts. Within the 16 rows of one device no expert is named more than 4 times, a bound that some block reaches there.
All inputs are finite; a program needn't handle non-finite values.
Results may differ from the reference program's by a relative error of at most 0.0058.
Values may be sent and summed in bfloat16 or wider, within the bound.
A program may use at most 64 MiB of HBM per device.

```python
import math
import jax
import jax.numpy as jnp
import numpy as np
from jax import lax

D = 4096
HID = 1536
TOP = 8
FF = 12288
TOK_W = 16
TOKENS = 1024
EXPERTS = 64
CAP = 4
N_WIDE = 64


def levels(own_key, shape, cuts, least, top_value):
    def one(dim, shards_of):
        heights = jax.random.uniform(jax.random.fold_in(jax.random.fold_in(own_key, 6), dim), (shards_of,), jnp.float32, least / len(cuts), top_value / len(cuts))
        return jnp.repeat(jnp.exp(heights), shape[dim] // shards_of).reshape((-1,) + (1,) * (len(shape) - dim - 1))

    factor_of = one(*cuts[0])
    for cut in cuts[1:]:
        factor_of = factor_of * one(*cut)
    return factor_of


def assign_block(own_key, own, number, rows, count, top, bound, slope):
    order = jax.random.permutation(own_key, count)
    packed, ordinary = load_shares(count, rows * top, bound, slope, True), load_shares(count, rows * top, bound, slope, False)
    places = jnp.arange(count)

    def named(sizes, rotation):
        used = int((sizes > 0).sum())
        fixed = max(1, used // 4)
        moved = fixed + (places - fixed + rotation * (used - fixed)) % max(1, count - fixed)
        return jnp.zeros((count,), jnp.int32).at[order[jnp.where(places < fixed, places, moved)]].set(jnp.asarray(sizes, jnp.int32))

    sizes = jnp.where(number % 4 == 0, named(packed, number // 4), named(ordinary, number - number // 4 - 1))
    mixed = jax.random.permutation(jax.random.fold_in(own, 3), count)
    donor, sink = mixed[0:count // 2 * 2:2], mixed[1:count // 2 * 2:2]
    margin = jnp.minimum(sizes[donor] - 1, bound - sizes[sink]) // 2
    margin = jnp.where((donor == order[0]) | (sink == order[0]) | (sizes[sink] == 0), 0, jnp.maximum(margin, 0))
    moved = jax.random.randint(jax.random.fold_in(own, 4), (count // 2,), 0, 1 << 20) % (margin + 1)
    sizes = sizes.at[donor].add(-moved).at[sink].add(moved)
    labels = jnp.searchsorted(jnp.cumsum(sizes), jnp.arange(rows * top), side="right").astype(jnp.int32)
    table = labels.reshape(top, rows).T
    table = table[jax.random.permutation(jax.random.fold_in(own, 1), rows)]
    rotation = jax.random.randint(jax.random.fold_in(own, 2), (rows, 1), 0, top)
    return jnp.take_along_axis(table, (jnp.arange(top)[None, :] + rotation) % top, axis=1)


def load_shares(count, total, bound, skew, full):
    portions = [(1 << 20) // math.isqrt(grade ** skew) + 1 for grade in range(1, count + 1)]
    largest = bound if full else min(bound, max(-(-total // count), total * portions[0] // sum(portions)))
    least = 1 if total - largest >= count - 1 else 0
    given, surplus = [largest] + [least] * (count - 1), total - largest - least * (count - 1)
    while surplus > 0:
        candidates = [i for i in range(1, count) if given[i] < largest] or [i for i in range(1, count) if given[i] < bound]
        whole, budget = sum([portions[i] for i in candidates]), surplus
        for i in candidates:
            addition = min(bound - given[i], max(1, budget * portions[i] // whole), surplus)
            given[i] = given[i] + addition
            surplus = surplus - addition
    return np.array(given)


def scatter_about(stream_key, shape, spread, limit, shards=(), held_as=jnp.bfloat16):
    values = spread * jax.random.normal(stream_key, shape, jnp.float32)
    if shards:
        values = values * levels(stream_key, shape, shards, -0.22, 0.18)
    return jnp.clip(values, -limit, limit).astype(held_as)


def setup_inputs(seed: int = 0) -> dict:
    keys = jax.random.split(jax.random.key(seed), 10)
    layer_in = scatter_about(keys[0], (TOKENS, D), 1.0, 6.0, ((0, 64), (1, 4)))
    route_ids_keys = jax.random.split(jax.random.fold_in(keys[1], 1), TOKENS // TOK_W)
    route_ids_turns = jax.random.permutation(jax.random.fold_in(keys[1], 3), TOKENS // TOK_W)
    route_ids = jax.vmap(lambda own, number: assign_block(jax.random.fold_in(keys[1], 2), own, number, TOK_W, EXPERTS, TOP, CAP, 1))(route_ids_keys, route_ids_turns).reshape((TOKENS, TOP))
    route_scores = jnp.clip(jnp.exp(math.log(1.0) - 2.9957323 * jax.random.uniform(keys[2], (TOKENS, TOP), jnp.float32) ** levels(keys[2], (TOKENS, TOP), ((0, 64),), -0.2, 0.2)), 0.05, 1.0)
    expert_gate = scatter_about(keys[3], (EXPERTS, HID, D), D ** -0.5, 0.09375, ((0, 64), (2, 4)))
    expert_up = scatter_about(keys[4], (EXPERTS, HID, D), D ** -0.5, 0.09375, ((0, 64), (2, 4)))
    expert_down = scatter_about(keys[5], (EXPERTS, HID, D), HID ** -0.5, 0.15625, ((0, 64), (2, 4)))
    student_gate = scatter_about(keys[6], (FF, D), D ** -0.5, 0.09375, ((0, 64), (1, 4)))
    student_up = scatter_about(keys[7], (FF, D), D ** -0.5, 0.09375, ((0, 64), (1, 4)))
    student_down = scatter_about(keys[8], (FF, D), FF ** -0.5, 0.0546875, ((0, 64), (1, 4)))
    return {"layer_in": layer_in, "route_ids": route_ids, "route_scores": route_scores, "expert_gate": expert_gate, "expert_up": expert_up, "expert_down": expert_down, "student_gate": student_gate, "student_up": student_up, "student_down": student_down}


def silu_terms(values):
    sig_value = jax.nn.sigmoid(values)
    return (values * sig_value, sig_value)

def reference(layer_in, route_ids, route_scores, expert_gate, expert_up, expert_down, student_gate, student_up, student_down):
    route_weights = route_scores / lax.optimization_barrier(jnp.sum(route_scores, axis=1, keepdims=True))
    flat_ids = route_ids.reshape(-1).astype(jnp.int32)
    flat_weights = route_weights.reshape(-1)
    flat_tokens = (jnp.arange(TOKENS * TOP, dtype=jnp.int32) // TOP).astype(jnp.int32)
    most_rows = N_WIDE * CAP

    def one_expert(running, pieces):
        number, gate_mat, up_mat, down_mat = pieces
        is_taken = flat_ids == number
        slot_order = jnp.cumsum(is_taken.astype(jnp.int32)) - 1
        target = jnp.where(is_taken, slot_order, most_rows).astype(jnp.int32)
        token_of = jnp.zeros((most_rows,), jnp.int32).at[target].set(flat_tokens, mode='drop')
        weight_of = jnp.zeros((most_rows,), jnp.float32).at[target].set(flat_weights, mode='drop')
        picked_rows = layer_in[token_of]
        gate_pre = jnp.dot(picked_rows, gate_mat.T, preferred_element_type=jnp.float32)
        up_pre = jnp.dot(picked_rows, up_mat.T, preferred_element_type=jnp.float32)
        swished, _ = silu_terms(gate_pre)
        expert_hidden = (swished * up_pre).astype(jnp.bfloat16)
        expert_value = jnp.dot(expert_hidden, down_mat, preferred_element_type=jnp.float32).astype(jnp.bfloat16)
        running = running.at[token_of].add(weight_of[:, None] * expert_value.astype(jnp.float32))
        return (running, None)
    start_sum = jnp.zeros((TOKENS, D), jnp.float32)
    numbers = jnp.arange(EXPERTS, dtype=jnp.int32)
    summed, _ = lax.scan(one_expert, start_sum, (numbers, expert_gate, expert_up, expert_down))
    teacher_out = summed.astype(jnp.bfloat16)
    gate_pre = jnp.dot(layer_in, student_gate.T, preferred_element_type=jnp.float32)
    up_pre = jnp.dot(layer_in, student_up.T, preferred_element_type=jnp.float32)
    swished, sig_value = silu_terms(gate_pre)
    student_hidden = (swished * up_pre).astype(jnp.bfloat16)
    student_out = jnp.dot(student_hidden, student_down, preferred_element_type=jnp.float32)
    loss_scale = 1.0 / math.sqrt(TOKENS)
    delta_rows = (student_out - summed) * loss_scale
    grad_down = jnp.dot(student_hidden.astype(jnp.float32).T, delta_rows, precision=lax.Precision.HIGHEST, preferred_element_type=jnp.float32).astype(jnp.bfloat16)
    hidden_grad = jnp.dot(delta_rows, student_down.astype(jnp.float32).T, precision=lax.Precision.HIGHEST, preferred_element_type=jnp.float32)
    gate_grad_pre = (hidden_grad * up_pre * sig_value * (1.0 + gate_pre * (1.0 - sig_value))).astype(jnp.bfloat16)
    up_grad_pre = (hidden_grad * swished).astype(jnp.bfloat16)
    grad_gate = jnp.dot(gate_grad_pre.T, layer_in, preferred_element_type=jnp.float32).astype(jnp.bfloat16)
    grad_up = jnp.dot(up_grad_pre.T, layer_in, preferred_element_type=jnp.float32).astype(jnp.bfloat16)
    return (teacher_out, grad_gate, grad_up, grad_down)
```

```python
import math

import jax
import jax.numpy as jnp
from jax import lax
from jax.sharding import PartitionSpec as P


def silu_terms(values):
    sig_value = jax.nn.sigmoid(values)
    return (values * sig_value, sig_value)


def pair_total(first_term, second_term):
    return lax.psum((first_term, second_term), "dp")


def against(left_mat, right_mat):
    return lax.dot_general(
        left_mat, right_mat, (((1,), (1,)), ((), ())), preferred_element_type=jnp.float32
    )


def across(left_mat, right_mat):
    return lax.dot_general(
        left_mat, right_mat, (((0,), (0,)), ((), ())), preferred_element_type=jnp.float32
    )


def precise_against(left_mat, right_mat):
    return lax.dot_general(
        left_mat,
        right_mat,
        (((1,), (1,)), ((), ())),
        precision=lax.Precision.HIGHEST,
        preferred_element_type=jnp.float32,
    )


def precise_across(left_mat, right_mat):
    return lax.dot_general(
        left_mat,
        right_mat,
        (((0,), (0,)), ((), ())),
        precision=lax.Precision.HIGHEST,
        preferred_element_type=jnp.float32,
    )


def shards(
    layer_in,
    route_ids,
    route_scores,
    expert_gate,
    expert_up,
    expert_down,
    student_gate,
    student_up,
    student_down,
):
    owners = lax.axis_size("wide")
    tok_rows, columns = layer_in.shape
    top_k = route_ids.shape[1]
    capacity = min(tok_rows, max(2, 2 * tok_rows * top_k // owners))
    slot_count = owners * capacity
    gate_mat = expert_gate[0]
    up_mat = expert_up[0]
    down_mat = expert_down[0]
    flat_ids = route_ids.reshape(-1)
    order = jnp.arange(flat_ids.shape[0], dtype=jnp.int32)
    same = (flat_ids[:, None] == flat_ids[None, :]) & (order[None, :] < order[:, None])
    slot_rank = jnp.sum(same.astype(jnp.int32), axis=1)
    slot_of = flat_ids * capacity + slot_rank
    placed = (slot_of[None, :] == jnp.arange(slot_count, dtype=jnp.int32)[:, None]).astype(
        jnp.float32
    )
    placed = placed.reshape(slot_count, tok_rows, top_k)
    picker = jnp.sum(placed, axis=2).astype(jnp.bfloat16)
    outgoing = jnp.dot(picker, layer_in, preferred_element_type=jnp.float32).astype(jnp.bfloat16)
    outgoing = outgoing.reshape(owners, capacity, columns)
    route_weights = route_scores / jnp.sum(route_scores, axis=1, keepdims=True)
    mix_table = jnp.sum(placed * route_weights[None, :, :], axis=2)
    arrived = lax.all_to_all(outgoing, "wide", split_axis=0, concat_axis=0, tiled=True)
    sources, slot_len, col_len = arrived.shape
    flat_rows = arrived.reshape(sources * slot_len, col_len)
    gate_part = against(flat_rows, gate_mat)
    up_part = against(flat_rows, up_mat)
    gate_share = lax.psum_scatter(gate_part, "dp", scatter_dimension=1, tiled=True)
    up_share = lax.psum_scatter(up_part, "dp", scatter_dimension=1, tiled=True)
    swished, _ = silu_terms(gate_share)
    expert_hidden = lax.all_gather(
        (swished * up_share).astype(jnp.bfloat16), "dp", axis=1, tiled=True
    )
    expert_value = jnp.dot(expert_hidden, down_mat, preferred_element_type=jnp.float32).astype(
        jnp.bfloat16
    )
    returned = lax.all_to_all(
        expert_value.reshape(sources, slot_len, col_len),
        "wide",
        split_axis=0,
        concat_axis=0,
        tiled=True,
    )
    returned = returned.reshape(slot_count, columns).astype(jnp.float32)
    mixed_rows = lax.dot_general(
        mix_table,
        returned,
        (((0,), (0,)), ((), ())),
        precision=lax.Precision.HIGHEST,
        preferred_element_type=jnp.float32,
    )
    gathered = lax.all_gather(layer_in, "wide", axis=0, tiled=True)
    gate_pre, up_pre = pair_total(against(gathered, student_gate), against(gathered, student_up))
    swished, sig_value = silu_terms(gate_pre)
    student_hidden = (swished * up_pre).astype(jnp.bfloat16)
    part_rows = student_hidden
    student_out = lax.psum_scatter(
        jnp.dot(part_rows, student_down, preferred_element_type=jnp.float32),
        "wide",
        scatter_dimension=0,
        tiled=True,
    )
    saved_state = (gathered, gate_pre, up_pre, swished, sig_value, student_hidden, student_out)
    teacher_out = mixed_rows.astype(jnp.bfloat16)
    gathered, gate_pre, up_pre, swished, sig_value, student_hidden, student_out = saved_state
    loss_scale = 1.0 / math.sqrt(tok_rows * owners)
    delta_rows = (student_out - mixed_rows) * loss_scale
    delta_all = lax.all_gather(delta_rows, "wide", axis=0, tiled=True)
    grad_down = precise_across(student_hidden.astype(jnp.float32), delta_all).astype(jnp.bfloat16)
    hidden_grad = lax.psum(precise_against(delta_all, student_down.astype(jnp.float32)), "dp")
    gate_grad_pre = (
        hidden_grad * up_pre * sig_value * (1.0 + gate_pre * (1.0 - sig_value))
    ).astype(jnp.bfloat16)
    up_grad_pre = (hidden_grad * swished).astype(jnp.bfloat16)
    grad_gate = across(gate_grad_pre, gathered).astype(jnp.bfloat16)
    grad_up = across(up_grad_pre, gathered).astype(jnp.bfloat16)
    return (teacher_out, grad_gate, grad_up, grad_down)


def solution(mesh):
    in_specs = (
        P("wide", "dp"),
        P("wide", None),
        P("wide", None),
        P("wide", None, "dp"),
        P("wide", None, "dp"),
        P("wide", None, "dp"),
        P("wide", "dp"),
        P("wide", "dp"),
        P("wide", "dp"),
    )
    out_specs = (P("wide", "dp"), P("wide", "dp"), P("wide", "dp"), P("wide", "dp"))
    return jax.shard_map(shards, mesh=mesh, in_specs=in_specs, out_specs=out_specs, check_vma=False)
```

```python
import math

import jax
import jax.numpy as jnp
from jax import lax
from jax.experimental import pallas as pl
from jax.experimental.pallas import tpu as pltpu
from jax.sharding import PartitionSpec as P

MESH = pl.DeviceIdType.MESH
NX, NZ, NY = 4, 8, 2
NWIDE = NX * NZ * NY
BF, F32 = jnp.bfloat16, jnp.float32
NEAR_FIRST = (0, 1, 7, 2, 6, 3, 5, 4)
FAR_FIRST = (4, 3, 5, 2, 6, 1, 7, 0)
DMA = pltpu.SemaphoreType.DMA


def rcopy(src, dst, send_sem, recv_sem, **where):
    return pltpu.make_async_remote_copy(
        src_ref=src, dst_ref=dst, send_sem=send_sem, recv_sem=recv_sem, device_id=where, device_id_type=MESH
    )


def place_of(w):
    return lax.div(w, NX * NZ), lax.rem(lax.div(w, NX), NZ), lax.rem(w, NX)


def wide_of(yh, z, x):
    return yh * (NX * NZ) + z * NX + x


def gather_body(block_ref, buf, sems, me):
    yh, z, x = me
    y_s, y_r, z_s, z_r, p_s, p_r, m_s, m_r, fp_s, fp_r, fm_s, fm_r = sems
    right, left, far = lax.rem(x + 1, NX), lax.rem(x + NX - 1, NX), lax.rem(x + 2, NX)
    to_right, to_left = wide_of(yh, z, right), wide_of(yh, z, left)
    own = buf.at[yh, z, x]
    y_copy = rcopy(block_ref, own, y_s, y_r, wide=wide_of(1 - yh, z, x))
    y_copy.start()
    buf[yh, z, x] = block_ref[...]
    y_copy.wait_recv()
    pending = [y_copy]
    chunk = buf.at[:, z, x]
    z_of = [lax.rem(z - dz + NZ, NZ) for dz in range(NZ)]
    z_copies = {}
    for dz in FAR_FIRST[:-1]:
        c = rcopy(chunk, chunk, z_s.at[dz], z_r.at[dz], wide=wide_of(yh, lax.rem(z + dz, NZ), x))
        c.start()
        pending.append(c)

    def spread(k):
        zc = z_of[NEAR_FIRST[k]]
        part = buf.at[:, zc, x]
        if k:
            dz = NEAR_FIRST[k]
            rcopy(part, part, z_s.at[dz], z_r.at[dz], wide=to_right).wait_recv()
        for s, r, to in ((p_s, p_r, to_right), (m_s, m_r, to_left)):
            c = rcopy(part, part, s.at[k], r.at[k], wide=to)
            c.start()
            pending.append(c)

    def forward(k):
        zc = z_of[NEAR_FIRST[k]]
        for s, r, fs, fr, side, half, to in (
            (p_s, p_r, fp_s, fp_r, left, 0, to_right),
            (m_s, m_r, fm_s, fm_r, right, 1, to_left),
        ):
            came = buf.at[:, zc, side]
            rcopy(came, came, s.at[k], r.at[k], wide=to).wait_recv()
            part = buf.at[half, zc, side]
            c = rcopy(part, part, fs.at[k], fr.at[k], wide=to)
            c.start()
            pending.append(c)

    for k in range(NZ + 1):
        if k < NZ:
            spread(k)
        if k >= 1:
            forward(k - 1)
    for k in range(NZ):
        zc = z_of[NEAR_FIRST[k]]
        for fs, fr, half in ((fp_s, fp_r, 0), (fm_s, fm_r, 1)):
            part = buf.at[half, zc, far]
            rcopy(part, part, fs.at[k], fr.at[k], wide=to_left).wait_recv()
    for c in pending:
        c.wait_send()


GATHER_SEMS = [DMA(()), DMA(())] + [DMA((NZ,)) for _ in range(10)]


def greet(peers):
    barrier = pltpu.get_barrier_semaphore()
    for peer in peers:
        pl.semaphore_signal(barrier, inc=1, device_id=peer, device_id_type=MESH)
    pl.semaphore_wait(barrier, len(peers))


def gather_peers(me):
    yh, z, x = me
    peers = [{"wide": wide_of(1 - yh, z, x)}]
    peers += [{"wide": wide_of(yh, lax.rem(z + dz, NZ), x)} for dz in range(1, NZ)]
    peers += [{"wide": wide_of(yh, z, lax.rem(x + dx, NX))} for dx in (1, NX - 1)]
    return peers


def gather_tokens_kernel(block_ref, x_out, id_out, buf, out_sem, *sems):
    me = place_of(lax.axis_index("wide"))
    greet(gather_peers(me))
    gather_body(block_ref, buf, sems, me)
    width = x_out.shape[-1]
    c = pltpu.make_async_copy(buf.at[:, :, :, :, pl.ds(0, width)], x_out, out_sem)
    c.start()
    id_out[...] = buf[:, :, :, :, width:]
    c.wait()


def gather_rows_kernel(block_ref, buf, *sems):
    me = place_of(lax.axis_index("wide"))
    greet(gather_peers(me))
    gather_body(block_ref, buf, sems, me)


def params(number):
    return pltpu.CompilerParams(collective_id=number, has_side_effects=True, vmem_limit_bytes=32 << 20)


VM = pl.BlockSpec(memory_space=pltpu.VMEM)
ANY = pl.BlockSpec(memory_space=pl.ANY)


def gather_tokens(block, width):
    rows, full = block.shape
    return pl.pallas_call(
        gather_tokens_kernel,
        out_shape=(
            jax.ShapeDtypeStruct((NY, NZ, NX, rows, width), BF),
            jax.ShapeDtypeStruct((NY, NZ, NX, rows, full - width), BF),
        ),
        in_specs=[VM],
        out_specs=(ANY, VM),
        scratch_shapes=[pltpu.VMEM((NY, NZ, NX, rows, full), BF), DMA(())] + GATHER_SEMS,
        compiler_params=params(0),
        name="gather_tokens",
    )(block)


def gather_rows(block):
    rows, width = block.shape
    return pl.pallas_call(
        gather_rows_kernel,
        out_shape=jax.ShapeDtypeStruct((NY, NZ, NX, rows, width), BF),
        in_specs=[VM],
        out_specs=VM,
        scratch_shapes=GATHER_SEMS,
        compiler_params=params(1),
        name="gather_delta",
    )(block)


def reduce_kernel(p_ref, v_ref, out_ref, ret_ref, ap, am, rp, rm, sp, sm, zs, zr, acc, yr, *sems):
    ap_s, ap_r, am_s, am_r, rp_s, rp_r, rm_s, rm_r, z_s, z_r, y_s, y_r, v_s, v_r = sems
    w = lax.axis_index("wide")
    yh, z, x = place_of(w)
    barrier = pltpu.get_barrier_semaphore()

    def hello(off, carry):
        pl.semaphore_signal(barrier, inc=1, device_id={"wide": lax.rem(w + off, NWIDE)}, device_id_type=MESH)
        return carry

    lax.fori_loop(1, NWIDE, hello, 0)
    pl.semaphore_wait(barrier, NWIDE - 1)
    right, left, far = lax.rem(x + 1, NX), lax.rem(x + NX - 1, NX), lax.rem(x + 2, NX)
    to_right, to_left = wide_of(yh, z, right), wide_of(yh, z, left)
    zc_of = [lax.rem(z + dz, NZ) for dz in FAR_FIRST]
    pending = []

    def go(c):
        c.start()
        pending.append(c)

    for k in range(NZ):
        go(rcopy(p_ref.at[0, zc_of[k], far], ap.at[k], ap_s.at[k], ap_r.at[k], wide=to_right))
        go(rcopy(p_ref.at[1, zc_of[k], far], am.at[k], am_s.at[k], am_r.at[k], wide=to_left))

    def values_copy(off):
        to = lax.rem(w + off, NWIDE)
        return rcopy(v_ref.at[to], ret_ref.at[w], v_s.at[off], v_r.at[off], wide=to)

    def send_values(off, carry):
        values_copy(off).start()
        return carry

    lax.fori_loop(1, NWIDE, send_values, 0)
    ret_ref[w] = v_ref[w]

    def merge(k):
        zc = zc_of[k]
        rcopy(ap.at[k], ap.at[k], ap_s.at[k], ap_r.at[k], wide=to_right).wait_recv()
        sp[k, 0] = (ap[k].astype(F32) + p_ref[0, zc, right].astype(F32)).astype(BF)
        sp[k, 1] = p_ref[1, zc, right]
        go(rcopy(sp.at[k], rp.at[k], rp_s.at[k], rp_r.at[k], wide=to_right))
        rcopy(am.at[k], am.at[k], am_s.at[k], am_r.at[k], wide=to_left).wait_recv()
        sm[k, 1] = (am[k].astype(F32) + p_ref[1, zc, left].astype(F32)).astype(BF)
        sm[k, 0] = p_ref[0, zc, left]
        go(rcopy(sm.at[k], rm.at[k], rm_s.at[k], rm_r.at[k], wide=to_left))

    def total(k):
        zc, dz = zc_of[k], FAR_FIRST[k]
        rcopy(rp.at[k], rp.at[k], rp_s.at[k], rp_r.at[k], wide=to_right).wait_recv()
        rcopy(rm.at[k], rm.at[k], rm_s.at[k], rm_r.at[k], wide=to_left).wait_recv()
        for h in range(NY):
            both = p_ref[h, zc, x].astype(F32) + rp[k, h].astype(F32) + rm[k, h].astype(F32)
            if dz == 0:
                acc[h] = both
            else:
                zs[k, h] = both.astype(BF)
        if dz:
            go(rcopy(zs.at[k], zr.at[dz], z_s.at[dz], z_r.at[dz], wide=wide_of(yh, zc, x)))

    for k in range(NZ + 1):
        if k < NZ:
            merge(k)
        if k >= 1:
            total(k - 1)
    for dz in FAR_FIRST[:-1]:
        rcopy(zr.at[dz], zr.at[dz], z_s.at[dz], z_r.at[dz], wide=to_right).wait_recv()
        for h in range(NY):
            acc[h] += zr[dz, h].astype(F32)
    y_copy = rcopy(acc.at[1 - yh], yr, y_s, y_r, wide=wide_of(1 - yh, z, x))
    go(y_copy)
    y_copy.wait_recv()
    out_ref[...] = acc[yh] + yr[...]

    def wait_values(off, carry):
        came = ret_ref.at[lax.rem(w - off + NWIDE, NWIDE)]
        rcopy(came, came, v_s.at[off], v_r.at[off], wide=to_right).wait_recv()
        values_copy(off).wait_send()
        return carry

    lax.fori_loop(1, NWIDE, wait_values, 0)
    for c in pending:
        c.wait_send()


def reduce_rows(partial, values):
    rows, width = partial.shape[-2:]
    return pl.pallas_call(
        reduce_kernel,
        out_shape=(jax.ShapeDtypeStruct((rows, width), F32), jax.ShapeDtypeStruct(values.shape, BF)),
        in_specs=[VM, VM],
        out_specs=(VM, VM),
        scratch_shapes=[
            pltpu.VMEM((NZ, rows, width), BF),
            pltpu.VMEM((NZ, rows, width), BF),
            pltpu.VMEM((NZ, NY, rows, width), BF),
            pltpu.VMEM((NZ, NY, rows, width), BF),
            pltpu.VMEM((NZ, NY, rows, width), BF),
            pltpu.VMEM((NZ, NY, rows, width), BF),
            pltpu.VMEM((NZ, NY, rows, width), BF),
            pltpu.VMEM((NZ, NY, rows, width), BF),
            pltpu.VMEM((NY, rows, width), F32),
            pltpu.VMEM((rows, width), F32),
        ]
        + [DMA((NZ,)) for _ in range(10)]
        + [DMA(()), DMA(()), DMA((NWIDE,)), DMA((NWIDE,))],
        compiler_params=params(2),
        name="reduce_student",
    )(partial, values)


def sum_over_dp(parts, bufs_a, stage, bufs_b, a_s, a_r, b_s, b_r, d):
    chip, core = lax.div(d, 2), lax.rem(d, 2)
    mate, across = chip * 2 + (1 - core), (1 - chip) * 2 + core
    pending = []
    for i, part in enumerate(parts):
        for j, q in ((0, (1 - chip) * 2 + (1 - core)), (1, mate)):
            c = rcopy(part.at[q], bufs_a[i].at[j], a_s.at[i, j], a_r.at[i, j], dp=mate)
            c.start()
            pending.append(c)
    for i, part in enumerate(parts):
        rcopy(bufs_a[i].at[0], bufs_a[i].at[0], a_s.at[i, 0], a_r.at[i, 0], dp=mate).wait_recv()
        stage[i][...] = (part[across] + bufs_a[i][0]).astype(BF)
        c = rcopy(stage[i], bufs_b[i], b_s.at[i], b_r.at[i], dp=across)
        c.start()
        pending.append(c)

    def finish(i):
        rcopy(bufs_a[i].at[1], bufs_a[i].at[1], a_s.at[i, 1], a_r.at[i, 1], dp=mate).wait_recv()
        rcopy(bufs_b[i], bufs_b[i], b_s.at[i], b_r.at[i], dp=across).wait_recv()
        return parts[i][d] + bufs_a[i][1] + bufs_b[i][...].astype(F32)

    return finish, pending


def share_over_dp(outs, y_s, y_r, m_s, m_r, d):
    chip, core = lax.div(d, 2), lax.rem(d, 2)
    mate, across = chip * 2 + (1 - core), (1 - chip) * 2 + core
    corner = (1 - chip) * 2 + (1 - core)
    pending = []

    def start(i):
        mine = outs[i].at[d]
        for s, r, to in ((y_s.at[i], y_r.at[i], across), (m_s.at[i, 0], m_r.at[i, 0], mate)):
            c = rcopy(mine, mine, s, r, dp=to)
            c.start()
            pending.append(c)

    def end():
        for i, out in enumerate(outs):
            came = out.at[across]
            rcopy(came, came, y_s.at[i], y_r.at[i], dp=across).wait_recv()
            c = rcopy(came, came, m_s.at[i, 1], m_r.at[i, 1], dp=mate)
            c.start()
            pending.append(c)
        for i, out in enumerate(outs):
            for j, q in ((0, mate), (1, corner)):
                rcopy(out.at[q], out.at[q], m_s.at[i, j], m_r.at[i, j], dp=mate).wait_recv()
        for c in pending:
            c.wait_send()

    return start, end


def dp_peers(d):
    chip, core = lax.div(d, 2), lax.rem(d, 2)
    return [{"dp": chip * 2 + (1 - core)}, {"dp": (1 - chip) * 2 + core}]


def forward_kernel(sg, su, eg, eu, hid, ehid, gate, up, *rest):
    bufs_a, stage, bufs_b = rest[0:4], rest[4:8], rest[8:12]
    a_s, a_r, b_s, b_r, y_s, y_r, m_s, m_r = rest[12:]
    d = lax.axis_index("dp")
    greet(dp_peers(d))
    finish, pending = sum_over_dp((sg, su, eg, eu), bufs_a, stage, bufs_b, a_s, a_r, b_s, b_r, d)
    start, end = share_over_dp((hid, ehid), y_s, y_r, m_s, m_r, d)
    g, u = finish(0), finish(1)
    gate[...] = g
    up[...] = u
    hid[d] = (g * jax.nn.sigmoid(g) * u).astype(BF)
    start(0)
    g, u = finish(2), finish(3)
    ehid[d] = (g * jax.nn.sigmoid(g) * u).astype(BF)
    start(1)
    end()
    for c in pending:
        c.wait_send()


def dp_scratch(parts):
    quarters = [p.shape[1:] for p in parts]
    return (
        [pltpu.VMEM((2,) + q, F32) for q in quarters]
        + [pltpu.VMEM(q, BF) for q in quarters]
        + [pltpu.VMEM(q, BF) for q in quarters]
    )


def dp_sems(n_parts, n_outs):
    return [
        DMA((n_parts, 2)),
        DMA((n_parts, 2)),
        DMA((n_parts,)),
        DMA((n_parts,)),
        DMA((n_outs,)),
        DMA((n_outs,)),
        DMA((n_outs, 2)),
        DMA((n_outs, 2)),
    ]


def forward_hidden(sg, su, eg, eu):
    parts = (sg, su, eg, eu)
    return pl.pallas_call(
        forward_kernel,
        out_shape=(
            jax.ShapeDtypeStruct(sg.shape, BF),
            jax.ShapeDtypeStruct(eg.shape, BF),
            jax.ShapeDtypeStruct(sg.shape[1:], F32),
            jax.ShapeDtypeStruct(sg.shape[1:], F32),
        ),
        in_specs=[VM] * 4,
        out_specs=(VM,) * 4,
        scratch_shapes=dp_scratch(parts) + dp_sems(4, 2),
        compiler_params=params(3),
        name="hidden_over_dp",
    )(*parts)


def backward_kernel(hg, gate, up, gg, ug, buf_a, stage, buf_b, a_s, a_r, b_s, b_r, y_s, y_r, m_s, m_r):
    d = lax.axis_index("dp")
    greet(dp_peers(d))
    finish, pending = sum_over_dp((hg,), (buf_a,), (stage,), (buf_b,), a_s, a_r, b_s, b_r, d)
    start, end = share_over_dp((gg, ug), y_s, y_r, m_s, m_r, d)
    g, u = gate[...], up[...]
    s = jax.nn.sigmoid(g)
    grad = finish(0)
    gg[d] = (grad * u * s * (1.0 + g * (1.0 - s))).astype(BF)
    start(0)
    ug[d] = (grad * (g * s)).astype(BF)
    start(1)
    end()
    for c in pending:
        c.wait_send()


def backward_hidden(hg, gate, up):
    return pl.pallas_call(
        backward_kernel,
        out_shape=(jax.ShapeDtypeStruct(hg.shape, BF), jax.ShapeDtypeStruct(hg.shape, BF)),
        in_specs=[VM] * 3,
        out_specs=(VM,) * 2,
        scratch_shapes=dp_scratch((hg,)) + dp_sems(1, 2),
        compiler_params=params(4),
        name="hidden_grad_over_dp",
    )(hg, gate, up)


def dot(a, b, dims, out=F32):
    return lax.dot_general(a, b, (dims, ((), ())), preferred_element_type=F32).astype(out)


def shards(
    layer_in,
    route_ids,
    route_scores,
    expert_gate,
    expert_up,
    expert_down,
    student_gate,
    student_up,
    student_down,
):
    tok_rows, columns = layer_in.shape
    top_k = route_ids.shape[1]
    owners = lax.axis_size("wide")
    cores = lax.axis_size("dp")
    capacity = 4
    slot_count = owners * capacity
    me = lax.axis_index("wide")
    tokens = owners * tok_rows
    hid = student_gate.shape[0]

    ids_cols = jnp.pad(route_ids.astype(BF), ((0, 0), (0, 128 - top_k)))
    gathered, ids_all = gather_tokens(jnp.concatenate([layer_in, ids_cols], axis=1), columns)
    gathered = gathered.reshape(tokens, columns)

    takes = jnp.any(ids_all.reshape(owners, tok_rows, 128)[:, :, :top_k] == me.astype(BF), axis=2)
    order = jnp.arange(tok_rows)
    earlier = (order[None, :] < order[:, None])[None, :, :] & takes[:, None, :]
    rank = jnp.sum(earlier.astype(jnp.int32), axis=2)
    slot_at = jnp.where(takes, rank + capacity * jnp.arange(owners)[:, None], slot_count).reshape(1, tokens)
    picker = (slot_at == jnp.arange(slot_count)[:, None]).astype(BF)
    rows = dot(picker, gathered, ((1,), (0,)), BF)

    gate_part = dot(student_gate, gathered, ((1,), (1,))).reshape(cores, hid // cores, tokens)
    up_part = dot(student_up, gathered, ((1,), (1,))).reshape(cores, hid // cores, tokens)
    e_hid = expert_gate.shape[1]
    e_gate = dot(rows, expert_gate[0], ((1,), (1,))).reshape(cores, slot_count // cores, e_hid)
    e_up = dot(rows, expert_up[0], ((1,), (1,))).reshape(cores, slot_count // cores, e_hid)
    hidden, e_hidden, gate_pre, up_pre = forward_hidden(gate_part, up_part, e_gate, e_up)
    hidden = hidden.reshape(hid, tokens)

    partial = dot(hidden, student_down, ((0,), (0,)), BF).reshape(NY, NZ, NX, tok_rows, columns)
    values = dot(e_hidden.reshape(slot_count, e_hid), expert_down[0], ((1,), (0,)), BF)
    student_out, returned = reduce_rows(partial, values.reshape(owners, capacity, columns))

    flat_ids = route_ids.reshape(-1)
    seq = jnp.arange(flat_ids.shape[0], dtype=jnp.int32)
    same = (flat_ids[:, None] == flat_ids[None, :]) & (seq[None, :] < seq[:, None])
    slot_of = (flat_ids * capacity + jnp.sum(same.astype(jnp.int32), axis=1)).reshape(tok_rows, top_k)
    weights = route_scores / jnp.sum(route_scores, axis=1, keepdims=True)
    mix = jnp.sum(
        jnp.where(slot_of[:, :, None] == jnp.arange(slot_count, dtype=jnp.int32), weights[:, :, None], 0.0), axis=1
    )
    teacher_sum = lax.dot_general(
        mix,
        returned.reshape(slot_count, columns).astype(F32),
        (((1,), (0,)), ((), ())),
        precision=lax.Precision.HIGHEST,
        preferred_element_type=F32,
    )
    delta = ((student_out - teacher_sum) * (1.0 / math.sqrt(tokens))).astype(BF)
    delta_all = gather_rows(delta).reshape(tokens, columns)

    hg = dot(student_down, delta_all, ((1,), (1,))).reshape(cores, hid // cores, tokens)
    gg, ug = backward_hidden(hg, gate_pre, up_pre)
    grad_down = dot(hidden, delta_all, ((1,), (0,)), BF)
    grad_gate = dot(gg.reshape(hid, tokens), gathered, ((1,), (0,)), BF)
    grad_up = dot(ug.reshape(hid, tokens), gathered, ((1,), (0,)), BF)
    return (teacher_sum.astype(BF), grad_gate, grad_up, grad_down)


def solution(mesh):
    in_specs = (
        P("wide", "dp"),
        P("wide", None),
        P("wide", None),
        P("wide", None, "dp"),
        P("wide", None, "dp"),
        P("wide", None, "dp"),
        P("wide", "dp"),
        P("wide", "dp"),
        P("wide", "dp"),
    )
    out_specs = (P("wide", "dp"), P("wide", "dp"), P("wide", "dp"), P("wide", "dp"))
    return jax.shard_map(shards, mesh=mesh, in_specs=in_specs, out_specs=out_specs, check_vma=False)
```

```python
import functools
import math

import jax
import jax.numpy as jnp
from jax import lax
from jax.experimental import pallas as pl
from jax.experimental.pallas import tpu as pltpu
from jax.sharding import PartitionSpec as P

MESH = pl.DeviceIdType.MESH
NX, NZ, NY = 4, 8, 2
NWIDE = NX * NZ * NY
BF, F32 = jnp.bfloat16, jnp.float32
NEAR_FIRST = (0, 1, 7, 2, 6, 3, 5, 4)
FAR_FIRST = (4, 3, 5, 2, 6, 1, 7)
DMA = pltpu.SemaphoreType.DMA


def rcopy(src, dst, send_sem, recv_sem, **where):
    return pltpu.make_async_remote_copy(
        src_ref=src, dst_ref=dst, send_sem=send_sem, recv_sem=recv_sem, device_id=where, device_id_type=MESH
    )


def place_of(w):
    return lax.div(w, NX * NZ), lax.rem(lax.div(w, NX), NZ), lax.rem(w, NX)


def wide_of(yh, z, x):
    return yh * (NX * NZ) + z * NX + x


def block_of(w):
    yh, z, x = place_of(w)
    return (z * NY + yh) * NX + x


def greet(peers):
    barrier = pltpu.get_barrier_semaphore()
    for peer in peers:
        pl.semaphore_signal(barrier, inc=1, device_id=peer, device_id_type=MESH)
    pl.semaphore_wait(barrier, len(peers))


def gather_peers(me):
    yh, z, x = me
    peers = [{"wide": wide_of(1 - yh, z, x)}]
    peers += [{"wide": wide_of(yh, lax.rem(z + dz, NZ), x)} for dz in range(1, NZ)]
    peers += [{"wide": wide_of(yh, z, lax.rem(x + dx, NX))} for dx in (1, NX - 1)]
    return peers


def dp_peers(d):
    chip, core = lax.div(d, 2), lax.rem(d, 2)
    return [{"dp": chip * 2 + (1 - core)}, {"dp": (1 - chip) * 2 + core}]


class Gather:
    sems = [DMA(()), DMA(())] + [DMA((NZ,)) for _ in range(10)]

    def __init__(self, buf, sems, me):
        self.buf, self.me, self.pending = buf, me, []
        self.y, self.zs, self.p, self.m, self.fp, self.fm = [sems[i : i + 2] for i in range(0, 12, 2)]
        yh, z, x = me
        self.right, self.left, self.far = lax.rem(x + 1, NX), lax.rem(x + NX - 1, NX), lax.rem(x + 2, NX)
        self.to_right, self.to_left = wide_of(yh, z, self.right), wide_of(yh, z, self.left)
        self.zc = [lax.rem(z - dz + NZ, NZ) for dz in NEAR_FIRST]

    def go(self, src, dst, sems, to, at=None):
        s, r = sems if at is None else (sems[0].at[at], sems[1].at[at])
        c = rcopy(src, dst, s, r, wide=to)
        c.start()
        self.pending.append(c)

    def got(self, ref, sems, at):
        rcopy(ref, ref, sems[0].at[at], sems[1].at[at], wide=self.to_right).wait_recv()

    def begin(self, block_ref):
        yh, z, x = self.me
        self.go(block_ref, self.buf.at[z, yh, x], self.y, wide_of(1 - yh, z, x))
        self.buf[z, yh, x] = block_ref[...]
        other = self.buf.at[z, 1 - yh, x]
        rcopy(other, other, *self.y, wide=self.to_right).wait_recv()
        chunk = self.buf.at[z, :, x]
        for dz in FAR_FIRST:
            self.go(chunk, chunk, self.zs, wide_of(yh, lax.rem(z + dz, NZ), x), dz)

    def spread(self, k):
        part = self.buf.at[self.zc[k], :, self.me[2]]
        if k:
            self.got(part, self.zs, NEAR_FIRST[k])
        self.go(part, part, self.p, self.to_right, k)
        self.go(part, part, self.m, self.to_left, k)

    def forward(self, k):
        for sems, onward, side, half, to in (
            (self.p, self.fp, self.left, 0, self.to_right),
            (self.m, self.fm, self.right, 1, self.to_left),
        ):
            self.got(self.buf.at[self.zc[k], :, side], sems, k)
            part = self.buf.at[self.zc[k], half, side]
            self.go(part, part, onward, to, k)

    def done(self, k):
        for onward, half in ((self.fp, 0), (self.fm, 1)):
            self.got(self.buf.at[self.zc[k], half, self.far], onward, k)

    def end(self):
        for c in self.pending:
            c.wait_send()


class Exchange:
    @staticmethod
    def scratch(n, slab, out_slab, across):
        return [
            pltpu.VMEM((n, 2, 2) + slab, F32),
            pltpu.VMEM((n, 2) + slab, F32),
            pltpu.VMEM((n,) + slab, across),
            pltpu.VMEM((n,) + slab, across),
            pltpu.VMEM((n, 4) + out_slab, BF),
        ] + [DMA((n,)) for _ in range(10)]

    def __init__(self, refs, d):
        self.parts, self.mated, self.stage, self.recv, self.out = refs[:5]
        self.a, self.b, self.y, self.m, self.f = [refs[i : i + 2] for i in range(5, 15, 2)]
        self.d, self.chip, self.core = d, lax.div(d, 2), lax.rem(d, 2)
        self.mate, self.across = self.chip * 2 + (1 - self.core), (1 - self.chip) * 2 + self.core
        self.corner = (1 - self.chip) * 2 + (1 - self.core)
        self.pending = []

    def go(self, src, dst, sems, k, to):
        c = rcopy(src, dst, sems[0].at[k], sems[1].at[k], dp=to)
        c.start()
        self.pending.append(c)

    def got(self, ref, sems, k):
        rcopy(ref, ref, sems[0].at[k], sems[1].at[k], dp=self.mate).wait_recv()

    def to_mate(self, k):
        self.go(self.parts.at[k, 1 - self.core], self.mated.at[k], self.a, k, self.mate)

    def to_across(self, k):
        self.got(self.mated.at[k], self.a, k)
        there = self.parts[k, self.core, 1 - self.chip] + self.mated[k, 1 - self.chip]
        self.stage[k] = there.astype(self.stage.dtype)
        self.go(self.stage.at[k], self.recv.at[k], self.b, k, self.across)

    def total(self, k):
        self.got(self.recv.at[k], self.b, k)
        return self.parts[k, self.core, self.chip] + self.mated[k, self.chip] + self.recv[k].astype(F32)

    def share(self, k):
        mine = self.out.at[k, self.d]
        self.go(mine, mine, self.y, k, self.across)
        self.go(mine, mine, self.m, k, self.mate)

    def pass_on(self, k):
        came = self.out.at[k, self.across]
        self.got(came, self.y, k)
        self.go(came, came, self.f, k, self.mate)

    def done(self, k):
        self.got(self.out.at[k, self.mate], self.m, k)
        self.got(self.out.at[k, self.corner], self.f, k)

    def end(self):
        for c in self.pending:
            c.wait_send()


class Reduce:
    @staticmethod
    def scratch(rows, width):
        return (
            [pltpu.VMEM((NZ, rows, width), BF)] * 2
            + [pltpu.VMEM((NZ, NY, rows, width), BF)] * 6
            + [pltpu.VMEM((NY, rows, width), F32), pltpu.VMEM((rows, width), F32)]
            + [DMA((NZ,)) for _ in range(10)]
            + [DMA(()), DMA(())]
        )

    def __init__(self, p, refs, g):
        self.p, self.g = p, g
        self.ap, self.am, self.rp, self.rm, self.sp, self.sm, self.zs, self.zr, self.acc, self.yr = refs[:10]
        self.s_ap, self.s_am, self.s_rp, self.s_rm, self.s_z, self.s_y = [refs[i : i + 2] for i in range(10, 22, 2)]

    def begin(self, k):
        g = self.g
        g.go(self.p.at[k, 0, g.far], self.ap.at[k], self.s_ap, g.to_right, k)
        g.go(self.p.at[k, 1, g.far], self.am.at[k], self.s_am, g.to_left, k)

    def merge(self, k):
        g, p = self.g, self.p
        g.got(self.ap.at[k], self.s_ap, k)
        self.sp[k, 0] = (self.ap[k].astype(F32) + p[k, 0, g.right].astype(F32)).astype(BF)
        self.sp[k, 1] = p[k, 1, g.right]
        g.go(self.sp.at[k], self.rp.at[k], self.s_rp, g.to_right, k)
        g.got(self.am.at[k], self.s_am, k)
        self.sm[k, 1] = (self.am[k].astype(F32) + p[k, 1, g.left].astype(F32)).astype(BF)
        self.sm[k, 0] = p[k, 0, g.left]
        g.go(self.sm.at[k], self.rm.at[k], self.s_rm, g.to_left, k)

    def total(self, k):
        g, dz = self.g, NEAR_FIRST[k]
        yh, z, x = g.me
        g.got(self.rp.at[k], self.s_rp, k)
        g.got(self.rm.at[k], self.s_rm, k)
        for h in range(NY):
            both = self.p[k, h, x].astype(F32) + self.rp[k, h].astype(F32) + self.rm[k, h].astype(F32)
            if dz == 0:
                self.acc[h] = both
            else:
                self.zs[k, h] = both.astype(BF)
        if dz:
            g.go(self.zs.at[k], self.zr.at[dz], self.s_z, wide_of(yh, g.zc[k], x), dz)

    def finish(self):
        g = self.g
        yh, z, x = g.me
        for dz in NEAR_FIRST[1:]:
            g.got(self.zr.at[dz], self.s_z, dz)
            for h in range(NY):
                self.acc[h] += self.zr[dz, h].astype(F32)
        g.go(self.acc.at[1 - yh], self.yr, self.s_y, wide_of(1 - yh, z, x))
        rcopy(self.yr, self.yr, *self.s_y, wide=g.to_right).wait_recv()
        return self.acc[yh] + self.yr[...]


def mm(a, b, dims):
    return lax.dot_general(a, b, (dims, ((), ())), preferred_element_type=F32)


E_TILE = 256


def forward_kernel(
    cols, rows_per, slots,
    block, s_gate, s_up, s_down, e_gate_h, e_up_h, e_down_h,
    x_out, hid_out, gate_out, up_out, out_ref, ret_ref,
    buf, e_gate, e_up, e_down, w_sem, x_sem, picked, p_ref, v_acc, v_ref, v_s, v_r, *rest,
):
    w, d = lax.axis_index("wide"), lax.axis_index("dp")
    me = place_of(w)
    loads = [
        pltpu.make_async_copy(src, dst, w_sem.at[i])
        for i, (src, dst) in enumerate(((e_gate_h, e_gate), (e_up_h, e_up), (e_down_h, e_down)))
    ]
    for c in loads:
        c.start()
    barrier = pltpu.get_barrier_semaphore()

    def hello(off, carry):
        pl.semaphore_signal(barrier, inc=1, device_id={"wide": lax.rem(w + off, NWIDE)}, device_id_type=MESH)
        return carry

    lax.fori_loop(1, NWIDE, hello, 0)
    for peer in dp_peers(d):
        pl.semaphore_signal(barrier, inc=1, device_id=peer, device_id_type=MESH)
    pl.semaphore_wait(barrier, NWIDE + 1)

    n_g, n_x, n_e = len(Gather.sems), 15, 15
    g = Gather(buf, rest[:n_g], me)
    st = Exchange(rest[n_g : n_g + n_x], d)
    ex = Exchange(rest[n_g + n_x : n_g + n_x + n_e], d)
    red = Reduce(p_ref, rest[n_g + n_x + n_e :], g)
    unit = s_gate.shape[0] // 4
    tok = NY * NX * rows_per
    tiles = e_gate.shape[0] // E_TILE
    quarter = slots // 4

    def lanes(k):
        return pl.ds(pl.multiple_of(g.zc[k] * tok, tok), tok)

    def student_a(k):
        g.done(k)
        xk = buf[g.zc[k], :, :, :, :cols].reshape(tok, cols)
        for i, weight in enumerate((s_gate, s_up)):
            part = mm(weight[...], xk, ((1,), (1,)))
            for q in range(4):
                st.parts[k, q % 2, q // 2, i] = part[q * unit : (q + 1) * unit]
        st.to_mate(k)

    def student_c(k):
        both = st.total(k)
        gate, up = both[0], both[1]
        gate_out[:, lanes(k)] = gate
        up_out[:, lanes(k)] = up
        st.out[k, d] = (gate * jax.nn.sigmoid(gate) * up).astype(BF)
        st.share(k)

    def student_e(k):
        st.done(k)
        hid = st.out[k].reshape(4 * unit, tok)
        hid_out[:, lanes(k)] = hid
        p_ref[k] = mm(hid, s_down[...], ((0,), (0,))).astype(BF).reshape(NY, NX, rows_per, cols)
        red.begin(k)

    def pick():
        lane = lax.broadcasted_iota(jnp.int32, (16, 128), 1)
        mine = jnp.where(lane == w, 1.0, 0.0).astype(BF)
        n_tok = tok * 2
        for half in range(NZ // 2):
            codes = buf[2 * half : 2 * half + 2, :, :, :, cols:].reshape(n_tok, 128)
            code = mm(mine, codes, ((1,), (1,)))[:1]
            at = 4 * lax.div(lax.broadcasted_iota(jnp.int32, (1, n_tok), 1), rows_per)
            slot = at.astype(F32) + code
            want = lax.broadcasted_iota(jnp.int32, (quarter, n_tok), 0).astype(F32)
            picker = jnp.where(slot == want, 1.0, 0.0).astype(BF)
            xs = buf[2 * half : 2 * half + 2, :, :, :, :cols].reshape(n_tok, cols)
            picked[quarter * half : quarter * (half + 1)] = mm(picker, xs, ((1,), (0,))).astype(BF)

    def expert_a(i):
        for j, weight in enumerate((e_gate, e_up)):
            part = mm(picked[...], weight[i * E_TILE : (i + 1) * E_TILE], ((1,), (1,)))
            for q in range(4):
                ex.parts[i, q % 2, q // 2, j] = part[q * quarter : (q + 1) * quarter]
        ex.to_mate(i)

    def expert_c(i):
        both = ex.total(i)
        gate, up = both[0], both[1]
        ex.out[i, d] = (gate * jax.nn.sigmoid(gate) * up).astype(BF)
        ex.share(i)

    def expert_e(i):
        ex.done(i)
        hid = ex.out[i].reshape(slots, E_TILE)
        more = mm(hid, e_down[i * E_TILE : (i + 1) * E_TILE], ((1,), (0,)))
        if i:
            v_acc[...] += more
        else:
            v_acc[...] = more

    def values_copy(off):
        to = lax.rem(w + off, NWIDE)
        return rcopy(v_ref.at[block_of(to)], ret_ref.at[w], v_s.at[off], v_r.at[off], wide=to)

    stages = [(g.spread, 0, NZ), (g.forward, 1, NZ), (student_a, 2, NZ), (st.to_across, 3, NZ), (student_c, 4, NZ)]
    stages += [(st.pass_on, 5, NZ), (student_e, 6, NZ), (red.merge, 7, NZ), (red.total, 8, NZ)]
    first = NZ + 2
    stages += [(expert_a, first, tiles), (ex.to_across, first + 1, tiles), (expert_c, first + 2, tiles)]
    stages += [(ex.pass_on, first + 3, tiles), (expert_e, first + 4, tiles)]
    g.begin(block)
    for t in range(first + 4 + tiles):
        if t == first:
            pltpu.make_async_copy(buf.at[:, :, :, :, pl.ds(0, cols)], x_out, x_sem).start()
            pick()
            loads[0].wait()
            loads[1].wait()
        if t == first + 4:
            loads[2].wait()
        for run, lag, count in stages:
            if 0 <= t - lag < count:
                run(t - lag)
    v_ref[...] = v_acc[...].reshape(v_ref.shape).astype(BF)
    lax.fori_loop(1, NWIDE, lambda off, c: (values_copy(off).start(), c)[1], 0)
    ret_ref[w] = v_ref[block_of(w)]
    out_ref[...] = red.finish()

    def wait_values(off, carry):
        came = ret_ref.at[lax.rem(w - off + NWIDE, NWIDE)]
        rcopy(came, came, v_s.at[off], v_r.at[off], wide=g.to_right).wait_recv()
        values_copy(off).wait_send()
        return carry

    lax.fori_loop(1, NWIDE, wait_values, 0)
    pltpu.make_async_copy(buf.at[:, :, :, :, pl.ds(0, cols)], x_out, x_sem).wait()
    g.end()
    st.end()
    ex.end()


VM = pl.BlockSpec(memory_space=pltpu.VMEM)
ANY = pl.BlockSpec(memory_space=pl.ANY)


def params(number):
    return pltpu.CompilerParams(collective_id=number, has_side_effects=True, vmem_limit_bytes=50 << 20)


def forward(block, s_gate, s_up, s_down, e_gate, e_up, e_down, slots):
    rows, full = block.shape
    hid, cols = s_gate.shape
    e_hid = e_gate.shape[0]
    unit, tok, tiles, quarter = hid // 4, NY * NX * rows, e_hid // E_TILE, slots // 4
    tokens = tok * NZ
    return pl.pallas_call(
        functools.partial(forward_kernel, cols, rows, slots),
        out_shape=(
            jax.ShapeDtypeStruct((NZ, NY, NX, rows, cols), BF),
            jax.ShapeDtypeStruct((hid, tokens), BF),
            jax.ShapeDtypeStruct((unit, tokens), F32),
            jax.ShapeDtypeStruct((unit, tokens), F32),
            jax.ShapeDtypeStruct((rows, cols), F32),
            jax.ShapeDtypeStruct((NWIDE, slots // NWIDE, cols), BF),
        ),
        in_specs=[VM] * 4 + [ANY] * 3,
        out_specs=(ANY, VM, VM, VM, VM, VM),
        scratch_shapes=[
            pltpu.VMEM((NZ, NY, NX, rows, full), BF),
            pltpu.VMEM((e_hid, cols), BF),
            pltpu.VMEM((e_hid, cols), BF),
            pltpu.VMEM((e_hid, cols), BF),
            DMA((3,)),
            DMA(()),
            pltpu.VMEM((slots, cols), BF),
            pltpu.VMEM((NZ, NY, NX, rows, cols), BF),
            pltpu.VMEM((slots, cols), F32),
            pltpu.VMEM((NWIDE, slots // NWIDE, cols), BF),
            DMA((NWIDE,)),
            DMA((NWIDE,)),
        ]
        + Gather.sems
        + Exchange.scratch(NZ, (2, unit, tok), (unit, tok), F32)
        + Exchange.scratch(tiles, (2, quarter, E_TILE), (quarter, E_TILE), BF)
        + Reduce.scratch(rows, cols),
        compiler_params=params(0),
        name="forward",
    )(block, s_gate, s_up, s_down, e_gate, e_up, e_down)


def backward_kernel(block, s_down, gate_ref, up_ref, buf, gg_out, ug_out, *rest):
    w, d = lax.axis_index("wide"), lax.axis_index("dp")
    me = place_of(w)
    greet(gather_peers(me) + dp_peers(d))
    n_g = len(Gather.sems)
    g = Gather(buf, rest[:n_g], me)
    ex = Exchange(rest[n_g:], d)
    unit, cols = s_down.shape[0] // 4, s_down.shape[1]
    tok = gate_ref.shape[1] // NZ

    def lanes(k):
        return pl.ds(pl.multiple_of(g.zc[k] * tok, tok), tok)

    def part(k):
        g.done(k)
        part = mm(s_down[...], buf[g.zc[k]].reshape(tok, cols), ((1,), (1,)))
        for q in range(4):
            ex.parts[k, q % 2, q // 2] = part[q * unit : (q + 1) * unit]
        ex.to_mate(k)

    def grads(k):
        grad = ex.total(k)
        gate, up = gate_ref[:, lanes(k)], up_ref[:, lanes(k)]
        s = jax.nn.sigmoid(gate)
        ex.out[k, d, 0] = (grad * up * s * (1.0 + gate * (1.0 - s))).astype(BF)
        ex.out[k, d, 1] = (grad * (gate * s)).astype(BF)
        ex.share(k)

    def store(k):
        ex.done(k)
        for q in range(4):
            gg_out[q * unit : (q + 1) * unit, lanes(k)] = ex.out[k, q, 0]
            ug_out[q * unit : (q + 1) * unit, lanes(k)] = ex.out[k, q, 1]

    stages = [(g.spread, 0), (g.forward, 1), (part, 2), (ex.to_across, 3), (grads, 4), (ex.pass_on, 5), (store, 6)]
    g.begin(block)
    for t in range(NZ + 6):
        for run, lag in stages:
            if 0 <= t - lag < NZ:
                run(t - lag)
    g.end()
    ex.end()


def backward(delta, s_down, gate, up):
    rows, cols = delta.shape
    hid = s_down.shape[0]
    unit, tokens = gate.shape
    return pl.pallas_call(
        backward_kernel,
        out_shape=(
            jax.ShapeDtypeStruct((NZ, NY, NX, rows, cols), BF),
            jax.ShapeDtypeStruct((hid, tokens), BF),
            jax.ShapeDtypeStruct((hid, tokens), BF),
        ),
        in_specs=[VM] * 4,
        out_specs=(VM,) * 3,
        scratch_shapes=Gather.sems + Exchange.scratch(NZ, (unit, tokens // NZ), (2, unit, tokens // NZ), F32),
        compiler_params=params(1),
        name="backward",
    )(delta, s_down, gate, up)


def dot(a, b, out=BF):
    return mm(a, b, ((1,), (0,))).astype(out)


def shards(
    layer_in,
    route_ids,
    route_scores,
    expert_gate,
    expert_up,
    expert_down,
    student_gate,
    student_up,
    student_down,
):
    tok_rows, columns = layer_in.shape
    top_k = route_ids.shape[1]
    owners = lax.axis_size("wide")
    capacity = 4
    slot_count = owners * capacity
    tokens = owners * tok_rows

    experts = jnp.arange(128, dtype=jnp.int32)
    takes = jnp.any(route_ids[:, :, None] == experts, axis=1)
    order = jnp.arange(tok_rows)
    earlier = order[None, :] < order[:, None]
    rank = jnp.sum(jnp.where(earlier[:, :, None] & takes[None, :, :], 1, 0), axis=1)
    codes = jnp.where(takes, rank, 4 * slot_count).astype(BF)

    gathered, hidden, gate_pre, up_pre, student_out, returned = forward(
        jnp.concatenate([layer_in, codes], axis=1),
        student_gate,
        student_up,
        student_down,
        expert_gate[0],
        expert_up[0],
        expert_down[0],
        slot_count,
    )

    weights = route_scores / jnp.sum(route_scores, axis=1, keepdims=True)
    code_of = jnp.sum(jnp.where(route_ids[:, :, None] == experts, rank[:, None, :], 0), axis=2)
    slot_of = route_ids * capacity + code_of
    mix = jnp.sum(
        jnp.where(slot_of[:, :, None] == jnp.arange(slot_count, dtype=jnp.int32), weights[:, :, None], 0.0), axis=1
    )
    teacher_sum = lax.dot_general(
        mix,
        returned.reshape(slot_count, columns).astype(F32),
        (((1,), (0,)), ((), ())),
        precision=lax.Precision.HIGHEST,
        preferred_element_type=F32,
    )
    delta = ((student_out - teacher_sum) * (1.0 / math.sqrt(tokens))).astype(BF)
    delta_all, gg, ug = backward(delta, student_down, gate_pre, up_pre)
    gathered = gathered.reshape(tokens, columns)
    grad_down = dot(hidden, delta_all.reshape(tokens, columns))
    grad_gate = dot(gg, gathered)
    grad_up = dot(ug, gathered)
    return (teacher_sum.astype(BF), grad_gate, grad_up, grad_down)


def solution(mesh):
    in_specs = (
        P("wide", "dp"),
        P("wide", None),
        P("wide", None),
        P("wide", None, "dp"),
        P("wide", None, "dp"),
        P("wide", None, "dp"),
        P("wide", "dp"),
        P("wide", "dp"),
        P("wide", "dp"),
    )
    out_specs = (P("wide", "dp"), P("wide", "dp"), P("wide", "dp"), P("wide", "dp"))
    return jax.shard_map(shards, mesh=mesh, in_specs=in_specs, out_specs=out_specs, check_vma=False)
```

```python
import functools
import math

import jax
import jax.numpy as jnp
from jax import lax
from jax.experimental import pallas as pl
from jax.experimental.pallas import tpu as pltpu
from jax.sharding import PartitionSpec as P

MESH = pl.DeviceIdType.MESH
NX, NZ, NY = 4, 8, 2
NWIDE = NX * NZ * NY
BF, F32 = jnp.bfloat16, jnp.float32
NEAR_FIRST = (0, 1, 7, 2, 6, 3, 5, 4)
DMA = pltpu.SemaphoreType.DMA


def rcopy(src, dst, send_sem, recv_sem, **where):
    return pltpu.make_async_remote_copy(
        src_ref=src, dst_ref=dst, send_sem=send_sem, recv_sem=recv_sem, device_id=where, device_id_type=MESH
    )


def place_of(w):
    return lax.div(w, NX * NZ), lax.rem(lax.div(w, NX), NZ), lax.rem(w, NX)


def wide_of(yh, z, x):
    return yh * (NX * NZ) + z * NX + x


def greet(peers):
    barrier = pltpu.get_barrier_semaphore()
    for peer in peers:
        pl.semaphore_signal(barrier, inc=1, device_id=peer, device_id_type=MESH)
    pl.semaphore_wait(barrier, len(peers))


def gather_peers(me):
    yh, z, x = me
    peers = [{"wide": wide_of(1 - yh, z, x)}]
    peers += [{"wide": wide_of(yh, lax.rem(z + dz, NZ), x)} for dz in range(1, NZ)]
    peers += [{"wide": wide_of(yh, z, lax.rem(x + dx, NX))} for dx in (1, NX - 1)]
    return peers


def dp_peers(d):
    chip, core = lax.div(d, 2), lax.rem(d, 2)
    return [{"dp": q} for q in (chip * 2 + (1 - core), (1 - chip) * 2 + core, (1 - chip) * 2 + (1 - core))]


class Gather:
    sems = [DMA(()), DMA(())] + [DMA((NZ,)) for _ in range(10)]

    def __init__(self, buf, sems, me):
        self.buf, self.me, self.pending = buf, me, []
        self.y, self.zs, self.p, self.m, self.fp, self.fm = [sems[i : i + 2] for i in range(0, 12, 2)]
        yh, z, x = me
        self.right, self.left, self.far = lax.rem(x + 1, NX), lax.rem(x + NX - 1, NX), lax.rem(x + 2, NX)
        self.to_right, self.to_left = wide_of(yh, z, self.right), wide_of(yh, z, self.left)
        self.zc = [lax.rem(z - dz + NZ, NZ) for dz in NEAR_FIRST]

    def go(self, src, dst, sems, to, at=None):
        s, r = sems if at is None else (sems[0].at[at], sems[1].at[at])
        c = rcopy(src, dst, s, r, wide=to)
        c.start()
        self.pending.append(c)

    def got(self, ref, sems, at):
        rcopy(ref, ref, sems[0].at[at], sems[1].at[at], wide=self.to_right).wait_recv()

    def begin(self, block_ref):
        yh, z, x = self.me
        self.go(block_ref, self.buf.at[z, yh, x], self.y, wide_of(1 - yh, z, x))
        self.buf[z, yh, x] = block_ref[...]
        other = self.buf.at[z, 1 - yh, x]
        rcopy(other, other, *self.y, wide=self.to_right).wait_recv()
        chunk = self.buf.at[z, :, x]
        for dz in NEAR_FIRST[1:]:
            self.go(chunk, chunk, self.zs, wide_of(yh, lax.rem(z + dz, NZ), x), dz)

    def spread(self, k):
        part = self.buf.at[self.zc[k], :, self.me[2]]
        if k:
            self.got(part, self.zs, NEAR_FIRST[k])
        self.go(part, part, self.p, self.to_right, k)
        self.go(part, part, self.m, self.to_left, k)

    def forward(self, k):
        for sems, onward, side, half, to in (
            (self.p, self.fp, self.left, 0, self.to_right),
            (self.m, self.fm, self.right, 1, self.to_left),
        ):
            self.got(self.buf.at[self.zc[k], :, side], sems, k)
            part = self.buf.at[self.zc[k], half, side]
            self.go(part, part, onward, to, k)

    def done(self, k):
        for onward, half in ((self.fp, 0), (self.fm, 1)):
            self.got(self.buf.at[self.zc[k], half, self.far], onward, k)

    def end(self):
        for c in self.pending:
            c.wait_send()


class Exchange:
    @staticmethod
    def scratch(n, slab, out_slab, across):
        return [
            pltpu.VMEM((n, 2, 2) + slab, F32),
            pltpu.VMEM((n, 2) + slab, F32),
            pltpu.VMEM((n,) + slab, across),
            pltpu.VMEM((n,) + slab, across),
            pltpu.VMEM((n, 4) + out_slab, BF),
        ] + [DMA((n,)) for _ in range(10)]

    def __init__(self, refs, d):
        self.parts, self.mated, self.stage, self.recv, self.out = refs[:5]
        self.a, self.b, self.y, self.m, self.f = [refs[i : i + 2] for i in range(5, 15, 2)]
        self.d, self.chip, self.core = d, lax.div(d, 2), lax.rem(d, 2)
        self.mate, self.across = self.chip * 2 + (1 - self.core), (1 - self.chip) * 2 + self.core
        self.corner = (1 - self.chip) * 2 + (1 - self.core)
        self.pending = []

    def go(self, src, dst, sems, k, to):
        c = rcopy(src, dst, sems[0].at[k], sems[1].at[k], dp=to)
        c.start()
        self.pending.append(c)

    def got(self, ref, sems, k):
        rcopy(ref, ref, sems[0].at[k], sems[1].at[k], dp=self.mate).wait_recv()

    def to_mate(self, k):
        self.go(self.parts.at[k, 1 - self.core], self.mated.at[k], self.a, k, self.mate)

    def to_across(self, k):
        self.got(self.mated.at[k], self.a, k)
        there = self.parts[k, self.core, 1 - self.chip] + self.mated[k, 1 - self.chip]
        self.stage[k] = there.astype(self.stage.dtype)
        self.go(self.stage.at[k], self.recv.at[k], self.b, k, self.across)

    def total(self, k):
        self.got(self.recv.at[k], self.b, k)
        return self.parts[k, self.core, self.chip] + self.mated[k, self.chip] + self.recv[k].astype(F32)

    def share(self, k):
        mine = self.out.at[k, self.d]
        self.go(mine, mine, self.y, k, self.across)
        self.go(mine, mine, self.m, k, self.mate)

    def pass_on(self, k):
        came = self.out.at[k, self.across]
        self.got(came, self.y, k)
        self.go(came, came, self.f, k, self.mate)

    def done(self, k):
        self.got(self.out.at[k, self.mate], self.m, k)
        self.got(self.out.at[k, self.corner], self.f, k)

    def end(self):
        for c in self.pending:
            c.wait_send()


class Direct:
    @staticmethod
    def scratch(n, slab, out_slab):
        return [
            pltpu.VMEM((n, 4) + slab, F32),
            pltpu.VMEM((n, 3) + slab, F32),
            pltpu.VMEM((n, 4) + out_slab, BF),
        ] + [DMA((3, n)) for _ in range(4)]

    def __init__(self, refs, d):
        self.parts, self.recv, self.out = refs[:3]
        self.a, self.b = refs[3:5], refs[5:7]
        chip, core = lax.div(d, 2), lax.rem(d, 2)
        self.d, self.pending = d, []
        self.peers = [chip * 2 + (1 - core), (1 - chip) * 2 + core, (1 - chip) * 2 + (1 - core)]

    def send(self, k):
        for j in (2, 1, 0):
            q = self.peers[j]
            c = rcopy(self.parts.at[k, q], self.recv.at[k, j], self.a[0].at[j, k], self.a[1].at[j, k], dp=q)
            c.start()
            self.pending.append(c)

    def total(self, k):
        whole = self.parts[k, self.d]
        for j in range(3):
            came = self.recv.at[k, j]
            rcopy(came, came, self.a[0].at[j, k], self.a[1].at[j, k], dp=self.peers[0]).wait_recv()
            whole = whole + self.recv[k, j]
        return whole

    def share(self, k):
        mine = self.out.at[k, self.d]
        for j in (2, 1, 0):
            c = rcopy(mine, mine, self.b[0].at[j, k], self.b[1].at[j, k], dp=self.peers[j])
            c.start()
            self.pending.append(c)

    def done(self, k):
        for j in range(3):
            came = self.out.at[k, self.peers[j]]
            rcopy(came, came, self.b[0].at[j, k], self.b[1].at[j, k], dp=self.peers[0]).wait_recv()

    def end(self):
        for c in self.pending:
            c.wait_send()


class Reduce:
    @staticmethod
    def scratch(rows, width):
        return (
            [pltpu.VMEM((NZ, rows, width), BF)] * 2
            + [pltpu.VMEM((NZ, NY, rows, width), BF)] * 6
            + [pltpu.VMEM((NY, rows, width), F32), pltpu.VMEM((rows, width), F32)]
            + [DMA((NZ,)) for _ in range(10)]
            + [DMA(()), DMA(())]
        )

    def __init__(self, p, refs, g):
        self.p, self.g = p, g
        self.ap, self.am, self.rp, self.rm, self.sp, self.sm, self.zs, self.zr, self.acc, self.yr = refs[:10]
        self.s_ap, self.s_am, self.s_rp, self.s_rm, self.s_z, self.s_y = [refs[i : i + 2] for i in range(10, 22, 2)]

    def begin(self, k):
        g = self.g
        g.go(self.p.at[k, 0, g.far], self.ap.at[k], self.s_ap, g.to_right, k)
        g.go(self.p.at[k, 1, g.far], self.am.at[k], self.s_am, g.to_left, k)

    def merge(self, k):
        g, p = self.g, self.p
        g.got(self.ap.at[k], self.s_ap, k)
        self.sp[k, 0] = (self.ap[k].astype(F32) + p[k, 0, g.right].astype(F32)).astype(BF)
        self.sp[k, 1] = p[k, 1, g.right]
        g.go(self.sp.at[k], self.rp.at[k], self.s_rp, g.to_right, k)
        g.got(self.am.at[k], self.s_am, k)
        self.sm[k, 1] = (self.am[k].astype(F32) + p[k, 1, g.left].astype(F32)).astype(BF)
        self.sm[k, 0] = p[k, 0, g.left]
        g.go(self.sm.at[k], self.rm.at[k], self.s_rm, g.to_left, k)

    def total(self, k):
        g, dz = self.g, NEAR_FIRST[k]
        yh, z, x = g.me
        g.got(self.rp.at[k], self.s_rp, k)
        g.got(self.rm.at[k], self.s_rm, k)
        for h in range(NY):
            both = self.p[k, h, x].astype(F32) + self.rp[k, h].astype(F32) + self.rm[k, h].astype(F32)
            if dz == 0:
                self.acc[h] = both
            else:
                self.zs[k, h] = both.astype(BF)
        if dz:
            g.go(self.zs.at[k], self.zr.at[dz], self.s_z, wide_of(yh, g.zc[k], x), dz)

    def finish(self):
        g = self.g
        yh, z, x = g.me
        for dz in NEAR_FIRST[1:]:
            g.got(self.zr.at[dz], self.s_z, dz)
            for h in range(NY):
                self.acc[h] += self.zr[dz, h].astype(F32)
        g.go(self.acc.at[1 - yh], self.yr, self.s_y, wide_of(1 - yh, z, x))
        rcopy(self.yr, self.yr, *self.s_y, wide=g.to_right).wait_recv()
        return self.acc[yh] + self.yr[...]


def mm(a, b, dims):
    return lax.dot_general(a, b, (dims, ((), ())), preferred_element_type=F32)


E_TILE = 512
BATCHES = 2


def forward_kernel(
    cols, rows_per, slots,
    block, s_gate_h, s_up_h, s_down_h, e_gate_h, e_up_h, e_down_h,
    x_out, hid_out, gate_out, up_out, out_ref, ret_ref,
    buf, s_gate, s_up, s_down, e_gate, e_up, e_down, w_sem, x_sem, picked, p_ref, v_acc, v_ref, v_s, v_r, *rest,
):
    w, d = lax.axis_index("wide"), lax.axis_index("dp")
    me = place_of(w)
    weights = ((s_gate_h, s_gate), (s_up_h, s_up), (s_down_h, s_down), (e_gate_h, e_gate), (e_up_h, e_up), (e_down_h, e_down))
    loads = [pltpu.make_async_copy(src, dst, w_sem.at[i]) for i, (src, dst) in enumerate(weights)]
    for c in loads:
        c.start()
    barrier = pltpu.get_barrier_semaphore()

    def hello(off, carry):
        pl.semaphore_signal(barrier, inc=1, device_id={"wide": lax.rem(w + off, NWIDE)}, device_id_type=MESH)
        return carry

    lax.fori_loop(1, NWIDE, hello, 0)
    for peer in dp_peers(d):
        pl.semaphore_signal(barrier, inc=1, device_id=peer, device_id_type=MESH)
    pl.semaphore_wait(barrier, NWIDE + 2)

    n_g, n_x, n_e = len(Gather.sems), 7, 15
    g = Gather(buf, rest[:n_g], me)
    st = Direct(rest[n_g : n_g + n_x], d)
    ex = Exchange(rest[n_g + n_x : n_g + n_x + n_e], d)
    red = Reduce(p_ref, rest[n_g + n_x + n_e :], g)
    unit = s_gate.shape[0] // 4
    tok = NY * NX * rows_per
    tiles = e_gate.shape[0] // E_TILE
    batch = slots // BATCHES
    quarter = batch // 4
    per_chunk = slots // NZ

    def lanes(k):
        return pl.ds(pl.multiple_of(g.zc[k] * tok, tok), tok)

    def student_a(k):
        g.done(k)
        xk = buf[g.zc[k], :, :, :, :cols].reshape(tok, cols)
        for i, weight in enumerate((s_gate, s_up)):
            part = mm(weight[...], xk, ((1,), (1,)))
            for q in range(4):
                st.parts[k, q, i] = part[q * unit : (q + 1) * unit]
        st.send(k)

    def student_c(k):
        both = st.total(k)
        gate, up = both[0], both[1]
        gate_out[:, lanes(k)] = gate
        up_out[:, lanes(k)] = up
        st.out[k, d] = (gate * jax.nn.sigmoid(gate) * up).astype(BF)
        st.share(k)

    def student_e(k):
        st.done(k)
        hid = st.out[k].reshape(4 * unit, tok)
        hid_out[:, lanes(k)] = hid
        p_ref[k] = mm(hid, s_down[...], ((0,), (0,))).astype(BF).reshape(NY, NX, rows_per, cols)
        red.begin(k)

    def pick(k):
        lane = lax.broadcasted_iota(jnp.int32, (16, 128), 1)
        mine = jnp.where(lane == w, 1.0, 0.0).astype(BF)
        code = mm(mine, buf[g.zc[k], :, :, :, cols:].reshape(tok, 128), ((1,), (1,)))[:1]
        at = 4 * lax.div(lax.broadcasted_iota(jnp.int32, (1, tok), 1), rows_per)
        want = lax.broadcasted_iota(jnp.int32, (per_chunk, tok), 0).astype(F32)
        picker = jnp.where(at.astype(F32) + code == want, 1.0, 0.0).astype(BF)
        xk = buf[g.zc[k], :, :, :, :cols].reshape(tok, cols)
        picked[per_chunk * k : per_chunk * (k + 1)] = mm(picker, xk, ((1,), (0,))).astype(BF)

    def expert_a(n):
        if n == 0:
            loads[3].wait()
            loads[4].wait()
        b, i = n // tiles, n % tiles
        for j, weight in enumerate((e_gate, e_up)):
            part = mm(picked[b * batch : (b + 1) * batch], weight[i * E_TILE : (i + 1) * E_TILE], ((1,), (1,)))
            for q in range(4):
                ex.parts[n, q % 2, q // 2, j] = part[q * quarter : (q + 1) * quarter]
        ex.to_mate(n)

    def expert_c(n):
        both = ex.total(n)
        gate, up = both[0], both[1]
        ex.out[n, d] = (gate * jax.nn.sigmoid(gate) * up).astype(BF)
        ex.share(n)

    def expert_e(n):
        if n == 0:
            loads[5].wait()
        b, i = n // tiles, n % tiles
        ex.done(n)
        more = mm(ex.out[n].reshape(batch, E_TILE), e_down[i * E_TILE : (i + 1) * E_TILE], ((1,), (0,)))
        if 0 < i < tiles - 1:
            v_acc[...] += more
        elif i == 0:
            v_acc[...] = more
        else:
            blocks = NWIDE // BATCHES
            v_ref[b * blocks : (b + 1) * blocks] = (v_acc[...] + more).reshape((blocks,) + v_ref.shape[1:]).astype(BF)
            for k in range(b * NZ // BATCHES, (b + 1) * NZ // BATCHES):
                lax.fori_loop(0 if k else 1, NY * NX, functools.partial(send_values, k), 0)

    yh, z, x = me

    def values_copy(k, j):
        to_y, to_x = lax.rem(yh + lax.div(j, NX), NY), lax.rem(x + lax.rem(j, NX), NX)
        at = k * NY * NX + j
        there = wide_of(to_y, g.zc[k], to_x)
        return rcopy(v_ref.at[k * NY * NX + to_y * NX + to_x], ret_ref.at[w], v_s.at[at], v_r.at[at], wide=there)

    def send_values(k, j, carry):
        values_copy(k, j).start()
        return carry

    def wait_values(k, j, carry):
        from_y, from_x = lax.rem(yh + NY - lax.div(j, NX), NY), lax.rem(x + NX - lax.rem(j, NX), NX)
        came = ret_ref.at[wide_of(from_y, lax.rem(z + NEAR_FIRST[k], NZ), from_x)]
        at = k * NY * NX + j
        rcopy(came, came, v_s.at[at], v_r.at[at], wide=g.to_right).wait_recv()
        values_copy(k, j).wait_send()
        return carry

    stages = [(g.spread, 0, NZ), (g.forward, 1, NZ), (student_a, 2, NZ), (student_c, 3, NZ), (student_e, 4, NZ)]
    stages += [(pick, 2, NZ), (red.merge, 5, NZ), (red.total, 6, NZ)]
    half = NZ // BATCHES
    experts = [(expert_a, 0), (ex.to_across, 1), (expert_c, 2), (ex.pass_on, 3), (expert_e, 4)]
    when = [half + 2 + i + b * half for b in range(BATCHES) for i in range(tiles)]
    g.begin(block)
    for c in loads[:3]:
        c.wait()
    for t in range(when[-1] + 5):
        if t == NZ + 2:
            pltpu.make_async_copy(buf.at[:, :, :, :, pl.ds(0, cols)], x_out, x_sem).start()
        for run, lag, count in stages:
            if 0 <= t - lag < count:
                run(t - lag)
        for run, lag in experts:
            if t - lag in when:
                run(when.index(t - lag))
    ret_ref[w] = v_ref[yh * NX + x]
    out_ref[...] = red.finish()
    for k in range(NZ):
        lax.fori_loop(0 if k else 1, NY * NX, functools.partial(wait_values, k), 0)
    pltpu.make_async_copy(buf.at[:, :, :, :, pl.ds(0, cols)], x_out, x_sem).wait()
    g.end()
    st.end()
    ex.end()


VM = pl.BlockSpec(memory_space=pltpu.VMEM)
ANY = pl.BlockSpec(memory_space=pl.ANY)


def params(number):
    return pltpu.CompilerParams(collective_id=number, has_side_effects=True, vmem_limit_bytes=50 << 20)


def forward(block, s_gate, s_up, s_down, e_gate, e_up, e_down, slots):
    rows, full = block.shape
    hid, cols = s_gate.shape
    e_hid = e_gate.shape[0]
    unit, tok, tiles, quarter = hid // 4, NY * NX * rows, e_hid // E_TILE, slots // 4 // BATCHES
    tokens = tok * NZ
    return pl.pallas_call(
        functools.partial(forward_kernel, cols, rows, slots),
        out_shape=(
            jax.ShapeDtypeStruct((NZ, NY, NX, rows, cols), BF),
            jax.ShapeDtypeStruct((hid, tokens), BF),
            jax.ShapeDtypeStruct((unit, tokens), F32),
            jax.ShapeDtypeStruct((unit, tokens), F32),
            jax.ShapeDtypeStruct((rows, cols), F32),
            jax.ShapeDtypeStruct((NWIDE, slots // NWIDE, cols), BF),
        ),
        in_specs=[VM] + [ANY] * 6,
        out_specs=(ANY, VM, VM, VM, VM, VM),
        scratch_shapes=[
            pltpu.VMEM((NZ, NY, NX, rows, full), BF),
        ]
        + [pltpu.VMEM((hid, cols), BF)] * 3
        + [pltpu.VMEM((e_hid, cols), BF)] * 3
        + [
            DMA((6,)),
            DMA(()),
            pltpu.VMEM((slots, cols), BF),
            pltpu.VMEM((NZ, NY, NX, rows, cols), BF),
            pltpu.VMEM((slots // BATCHES, cols), F32),
            pltpu.VMEM((NWIDE, slots // NWIDE, cols), BF),
            DMA((NWIDE,)),
            DMA((NWIDE,)),
        ]
        + Gather.sems
        + Direct.scratch(NZ, (2, unit, tok), (unit, tok))
        + Exchange.scratch(tiles * BATCHES, (2, quarter, E_TILE), (quarter, E_TILE), BF)
        + Reduce.scratch(rows, cols),
        compiler_params=params(0),
        name="forward",
    )(block, s_gate, s_up, s_down, e_gate, e_up, e_down)


def backward_kernel(block, s_down, gate_ref, up_ref, buf, gg_out, ug_out, *rest):
    w, d = lax.axis_index("wide"), lax.axis_index("dp")
    me = place_of(w)
    greet(gather_peers(me) + dp_peers(d))
    n_g = len(Gather.sems)
    g = Gather(buf, rest[:n_g], me)
    ex = Direct(rest[n_g:], d)
    unit, cols = s_down.shape[0] // 4, s_down.shape[1]
    tok = gate_ref.shape[1] // NZ

    def lanes(k):
        return pl.ds(pl.multiple_of(g.zc[k] * tok, tok), tok)

    def part(k):
        g.done(k)
        part = mm(s_down[...], buf[g.zc[k]].reshape(tok, cols), ((1,), (1,)))
        for q in range(4):
            ex.parts[k, q] = part[q * unit : (q + 1) * unit]
        ex.send(k)

    def grads(k):
        grad = ex.total(k)
        gate, up = gate_ref[:, lanes(k)], up_ref[:, lanes(k)]
        s = jax.nn.sigmoid(gate)
        ex.out[k, d, 0] = (grad * up * s * (1.0 + gate * (1.0 - s))).astype(BF)
        ex.out[k, d, 1] = (grad * (gate * s)).astype(BF)
        ex.share(k)

    def store(k):
        ex.done(k)
        for q in range(4):
            gg_out[q * unit : (q + 1) * unit, lanes(k)] = ex.out[k, q, 0]
            ug_out[q * unit : (q + 1) * unit, lanes(k)] = ex.out[k, q, 1]

    stages = [(g.spread, 0), (g.forward, 1), (part, 2), (grads, 3), (store, 4)]
    g.begin(block)
    for t in range(NZ + 4):
        for run, lag in stages:
            if 0 <= t - lag < NZ:
                run(t - lag)
    g.end()
    ex.end()


def backward(delta, s_down, gate, up):
    rows, cols = delta.shape
    hid = s_down.shape[0]
    unit, tokens = gate.shape
    return pl.pallas_call(
        backward_kernel,
        out_shape=(
            jax.ShapeDtypeStruct((NZ, NY, NX, rows, cols), BF),
            jax.ShapeDtypeStruct((hid, tokens), BF),
            jax.ShapeDtypeStruct((hid, tokens), BF),
        ),
        in_specs=[VM] * 4,
        out_specs=(VM,) * 3,
        scratch_shapes=Gather.sems + Direct.scratch(NZ, (unit, tokens // NZ), (2, unit, tokens // NZ)),
        compiler_params=params(1),
        name="backward",
    )(delta, s_down, gate, up)


def dot(a, b, out=BF):
    return mm(a, b, ((1,), (0,))).astype(out)


def shards(
    layer_in,
    route_ids,
    route_scores,
    expert_gate,
    expert_up,
    expert_down,
    student_gate,
    student_up,
    student_down,
):
    tok_rows, columns = layer_in.shape
    top_k = route_ids.shape[1]
    owners = lax.axis_size("wide")
    capacity = 4
    slot_count = owners * capacity
    tokens = owners * tok_rows

    experts = jnp.arange(128, dtype=jnp.int32)
    takes = jnp.any(route_ids[:, :, None] == experts, axis=1)
    order = jnp.arange(tok_rows)
    earlier = order[None, :] < order[:, None]
    rank = jnp.sum(jnp.where(earlier[:, :, None] & takes[None, :, :], 1, 0), axis=1)
    codes = jnp.where(takes, rank, 4 * slot_count).astype(BF)

    gathered, hidden, gate_pre, up_pre, student_out, returned = forward(
        jnp.concatenate([layer_in, codes], axis=1),
        student_gate,
        student_up,
        student_down,
        expert_gate[0],
        expert_up[0],
        expert_down[0],
        slot_count,
    )

    weights = route_scores / jnp.sum(route_scores, axis=1, keepdims=True)
    code_of = jnp.sum(jnp.where(route_ids[:, :, None] == experts, rank[:, None, :], 0), axis=2)
    slot_of = route_ids * capacity + code_of
    mix = jnp.sum(
        jnp.where(slot_of[:, :, None] == jnp.arange(slot_count, dtype=jnp.int32), weights[:, :, None], 0.0), axis=1
    )
    teacher_sum = lax.dot_general(
        mix,
        returned.reshape(slot_count, columns).astype(F32),
        (((1,), (0,)), ((), ())),
        precision=lax.Precision.HIGHEST,
        preferred_element_type=F32,
    )
    delta = ((student_out - teacher_sum) * (1.0 / math.sqrt(tokens))).astype(BF)
    delta_all, gg, ug = backward(delta, student_down, gate_pre, up_pre)
    gathered = gathered.reshape(tokens, columns)
    grad_down = dot(hidden, delta_all.reshape(tokens, columns))
    grad_gate = dot(gg, gathered)
    grad_up = dot(ug, gathered)
    return (teacher_sum.astype(BF), grad_gate, grad_up, grad_down)


def solution(mesh):
    in_specs = (
        P("wide", "dp"),
        P("wide", None),
        P("wide", None),
        P("wide", None, "dp"),
        P("wide", None, "dp"),
        P("wide", None, "dp"),
        P("wide", "dp"),
        P("wide", "dp"),
        P("wide", "dp"),
    )
    out_specs = (P("wide", "dp"), P("wide", "dp"), P("wide", "dp"), P("wide", "dp"))
    return jax.shard_map(shards, mesh=mesh, in_specs=in_specs, out_specs=out_specs, check_vma=False)
```

```python
import functools
import itertools
import math

import jax
import jax.numpy as jnp
from jax import lax
from jax.experimental import pallas as pl
from jax.experimental.pallas import tpu as pltpu
from jax.sharding import PartitionSpec as P

MESH = pl.DeviceIdType.MESH
NX, NZ, NY = 4, 8, 2
NWIDE = NX * NZ * NY
BF, F32 = jnp.bfloat16, jnp.float32
NEAR_FIRST = (0, 1, 7, 2, 6, 3, 5, 4)
DMA = pltpu.SemaphoreType.DMA


def rcopy(src, dst, send_sem, recv_sem, **where):
    return pltpu.make_async_remote_copy(
        src_ref=src, dst_ref=dst, send_sem=send_sem, recv_sem=recv_sem, device_id=where, device_id_type=MESH
    )


def place_of(w):
    return lax.div(w, NX * NZ), lax.rem(lax.div(w, NX), NZ), lax.rem(w, NX)


def wide_of(yh, z, x):
    return yh * (NX * NZ) + z * NX + x


def dp_peers(d):
    chip, core = lax.div(d, 2), lax.rem(d, 2)
    return [{"dp": q} for q in (chip * 2 + (1 - core), (1 - chip) * 2 + core, (1 - chip) * 2 + (1 - core))]


class Gather:
    sems = [DMA(()), DMA(())] + [DMA((NZ,)) for _ in range(10)]

    def __init__(self, buf, sems, me):
        self.buf, self.me, self.pending = buf, me, []
        self.y, self.zs, self.p, self.m, self.fp, self.fm = [sems[i : i + 2] for i in range(0, 12, 2)]
        yh, z, x = me
        self.right, self.left, self.far = lax.rem(x + 1, NX), lax.rem(x + NX - 1, NX), lax.rem(x + 2, NX)
        self.to_right, self.to_left = wide_of(yh, z, self.right), wide_of(yh, z, self.left)
        self.zc = [lax.rem(z - dz + NZ, NZ) for dz in NEAR_FIRST]

    def go(self, src, dst, sems, to, at=None):
        s, r = sems if at is None else (sems[0].at[at], sems[1].at[at])
        c = rcopy(src, dst, s, r, wide=to)
        c.start()
        self.pending.append(c)

    def got(self, ref, sems, at):
        rcopy(ref, ref, sems[0].at[at], sems[1].at[at], wide=self.to_right).wait_recv()

    def begin(self, block_ref):
        yh, z, x = self.me
        self.go(block_ref, self.buf.at[z, yh, x], self.y, wide_of(1 - yh, z, x))
        self.buf[z, yh, x] = block_ref[...]
        other = self.buf.at[z, 1 - yh, x]
        rcopy(other, other, *self.y, wide=self.to_right).wait_recv()
        chunk = self.buf.at[z, :, x]
        for dz in NEAR_FIRST[1:]:
            self.go(chunk, chunk, self.zs, wide_of(yh, lax.rem(z + dz, NZ), x), dz)

    def spread(self, k):
        part = self.buf.at[self.zc[k], :, self.me[2]]
        if k:
            self.got(part, self.zs, NEAR_FIRST[k])
        self.go(part, part, self.p, self.to_right, k)
        self.go(part, part, self.m, self.to_left, k)

    def forward(self, k):
        for sems, onward, side, half, to in (
            (self.p, self.fp, self.left, 0, self.to_right),
            (self.m, self.fm, self.right, 1, self.to_left),
        ):
            self.got(self.buf.at[self.zc[k], :, side], sems, k)
            part = self.buf.at[self.zc[k], half, side]
            self.go(part, part, onward, to, k)

    def done(self, k):
        for onward, half in ((self.fp, 0), (self.fm, 1)):
            self.got(self.buf.at[self.zc[k], half, self.far], onward, k)

    def end(self):
        for c in self.pending:
            c.wait_send()


class Exchange:
    @staticmethod
    def scratch(n, slab, out_slab, across):
        return [
            pltpu.VMEM((n, 2, 2) + slab, F32),
            pltpu.VMEM((n, 2) + slab, F32),
            pltpu.VMEM((n,) + slab, across),
            pltpu.VMEM((n,) + slab, across),
            pltpu.VMEM((n, 4) + out_slab, BF),
        ] + [DMA((n,)) for _ in range(10)]

    def __init__(self, refs, d):
        self.parts, self.mated, self.stage, self.recv, self.out = refs[:5]
        self.a, self.b, self.y, self.m, self.f = [refs[i : i + 2] for i in range(5, 15, 2)]
        self.d, self.chip, self.core = d, lax.div(d, 2), lax.rem(d, 2)
        self.mate, self.across = self.chip * 2 + (1 - self.core), (1 - self.chip) * 2 + self.core
        self.corner = (1 - self.chip) * 2 + (1 - self.core)
        self.pending = []

    def go(self, src, dst, sems, k, to):
        c = rcopy(src, dst, sems[0].at[k], sems[1].at[k], dp=to)
        c.start()
        self.pending.append(c)

    def got(self, ref, sems, k):
        rcopy(ref, ref, sems[0].at[k], sems[1].at[k], dp=self.mate).wait_recv()

    def to_mate(self, k):
        self.go(self.parts.at[k, 1 - self.core], self.mated.at[k], self.a, k, self.mate)

    def to_across(self, k):
        self.got(self.mated.at[k], self.a, k)
        there = self.parts[k, self.core, 1 - self.chip] + self.mated[k, 1 - self.chip]
        self.stage[k] = there.astype(self.stage.dtype)
        self.go(self.stage.at[k], self.recv.at[k], self.b, k, self.across)

    def total(self, k):
        self.got(self.recv.at[k], self.b, k)
        return self.parts[k, self.core, self.chip] + self.mated[k, self.chip] + self.recv[k].astype(F32)

    def share(self, k):
        mine = self.out.at[k, self.d]
        self.go(mine, mine, self.y, k, self.across)
        self.go(mine, mine, self.m, k, self.mate)

    def pass_on(self, k):
        came = self.out.at[k, self.across]
        self.got(came, self.y, k)
        self.go(came, came, self.f, k, self.mate)

    def done(self, k):
        self.got(self.out.at[k, self.mate], self.m, k)
        self.got(self.out.at[k, self.corner], self.f, k)

    def end(self):
        for c in self.pending:
            c.wait_send()


class Direct:
    @staticmethod
    def scratch(n, slab, out_slab):
        return [
            pltpu.VMEM((n, 4) + slab, F32),
            pltpu.VMEM((n, 3) + slab, F32),
            pltpu.VMEM((n, 4) + out_slab, BF),
        ] + [DMA((3, n)) for _ in range(4)]

    def __init__(self, refs, d):
        self.parts, self.recv, self.out = refs[:3]
        self.a, self.b = refs[3:5], refs[5:7]
        chip, core = lax.div(d, 2), lax.rem(d, 2)
        self.d, self.pending = d, []
        self.peers = [chip * 2 + (1 - core), (1 - chip) * 2 + core, (1 - chip) * 2 + (1 - core)]

    def send(self, k):
        for j in (2, 1, 0):
            q = self.peers[j]
            c = rcopy(self.parts.at[k, q], self.recv.at[k, j], self.a[0].at[j, k], self.a[1].at[j, k], dp=q)
            c.start()
            self.pending.append(c)

    def total(self, k):
        whole = self.parts[k, self.d]
        for j in range(3):
            came = self.recv.at[k, j]
            rcopy(came, came, self.a[0].at[j, k], self.a[1].at[j, k], dp=self.peers[0]).wait_recv()
            whole = whole + self.recv[k, j]
        return whole

    def share(self, k):
        mine = self.out.at[k, self.d]
        for j in (2, 1, 0):
            c = rcopy(mine, mine, self.b[0].at[j, k], self.b[1].at[j, k], dp=self.peers[j])
            c.start()
            self.pending.append(c)

    def done(self, k):
        for j in range(3):
            came = self.out.at[k, self.peers[j]]
            rcopy(came, came, self.b[0].at[j, k], self.b[1].at[j, k], dp=self.peers[0]).wait_recv()

    def end(self):
        for c in self.pending:
            c.wait_send()


class Reduce:
    @staticmethod
    def scratch(rows, width):
        return (
            [pltpu.VMEM((NZ, rows, width), BF)] * 2
            + [pltpu.VMEM((NZ, NY, rows, width), BF)] * 6
            + [pltpu.VMEM((NY, rows, width), F32), pltpu.VMEM((rows, width), F32)]
            + [DMA((NZ,)) for _ in range(10)]
            + [DMA(()), DMA(())]
        )

    def __init__(self, p, refs, g):
        self.p, self.g = p, g
        self.ap, self.am, self.rp, self.rm, self.sp, self.sm, self.zs, self.zr, self.acc, self.yr = refs[:10]
        self.s_ap, self.s_am, self.s_rp, self.s_rm, self.s_z, self.s_y = [refs[i : i + 2] for i in range(10, 22, 2)]

    def begin(self, k):
        g = self.g
        g.go(self.p.at[k, 0, g.far], self.ap.at[k], self.s_ap, g.to_right, k)
        g.go(self.p.at[k, 1, g.far], self.am.at[k], self.s_am, g.to_left, k)

    def merge(self, k):
        g, p = self.g, self.p
        g.got(self.ap.at[k], self.s_ap, k)
        self.sp[k, 0] = (self.ap[k].astype(F32) + p[k, 0, g.right].astype(F32)).astype(BF)
        self.sp[k, 1] = p[k, 1, g.right]
        g.go(self.sp.at[k], self.rp.at[k], self.s_rp, g.to_right, k)
        g.got(self.am.at[k], self.s_am, k)
        self.sm[k, 1] = (self.am[k].astype(F32) + p[k, 1, g.left].astype(F32)).astype(BF)
        self.sm[k, 0] = p[k, 0, g.left]
        g.go(self.sm.at[k], self.rm.at[k], self.s_rm, g.to_left, k)

    def total(self, k):
        g, dz = self.g, NEAR_FIRST[k]
        yh, z, x = g.me
        g.got(self.rp.at[k], self.s_rp, k)
        g.got(self.rm.at[k], self.s_rm, k)
        for h in range(NY):
            both = self.p[k, h, x].astype(F32) + self.rp[k, h].astype(F32) + self.rm[k, h].astype(F32)
            if dz == 0:
                self.acc[h] = both
            else:
                self.zs[k, h] = both.astype(BF)
        if dz:
            g.go(self.zs.at[k], self.zr.at[dz], self.s_z, wide_of(yh, g.zc[k], x), dz)

    def finish(self):
        g = self.g
        yh, z, x = g.me
        for dz in NEAR_FIRST[1:]:
            g.got(self.zr.at[dz], self.s_z, dz)
            for h in range(NY):
                self.acc[h] += self.zr[dz, h].astype(F32)
        g.go(self.acc.at[1 - yh], self.yr, self.s_y, wide_of(1 - yh, z, x))
        rcopy(self.yr, self.yr, *self.s_y, wide=g.to_right).wait_recv()
        return self.acc[yh] + self.yr[...]


def mm(a, b, dims):
    return lax.dot_general(a, b, (dims, ((), ())), preferred_element_type=F32)


E_TILE = 512
BATCHES = 2


def routes(ids, scores, slots):
    rows, top_k = ids.shape
    lane = lax.broadcasted_iota(jnp.int32, (rows, 128), 1)
    takes = jnp.zeros((rows, 128), F32)
    for k in range(top_k):
        takes += jnp.where(ids[:, k : k + 1] == lane, 1.0, 0.0)
    row, col = (lax.broadcasted_iota(jnp.int32, (rows, rows), a) for a in (0, 1))
    rank = mm(jnp.where(col < row, 1.0, 0.0).astype(BF), takes.astype(BF), ((1,), (0,)))
    codes = jnp.where(takes > 0.5, rank, 4.0 * slots).astype(BF)
    spread = lax.div(lax.broadcasted_iota(jnp.int32, (128, slots), 1), 4)
    spread = jnp.where(lax.broadcasted_iota(jnp.int32, (128, slots), 0) == spread, 1.0, 0.0).astype(BF)
    code_at = mm(codes, spread, ((1,), (0,)))
    slot = lax.broadcasted_iota(jnp.int32, (rows, slots), 1)
    expert = lax.div(slot, 4)
    weights = scores / jnp.sum(scores, axis=1, keepdims=True)
    weight_at = jnp.zeros((rows, slots), F32)
    for k in range(top_k):
        weight_at += jnp.where(ids[:, k : k + 1] == expert, weights[:, k : k + 1], 0.0)
    left = jnp.where(code_at == (slot - 4 * expert).astype(F32), weight_at, 0.0)
    terms = []
    for _ in range(3):
        terms.append(left.astype(BF))
        left = left - terms[-1].astype(F32)
    return codes, jnp.concatenate(terms, axis=0)


def step_kernel(
    cols, rows_per, slots,
    layer_in, ids_ref, scores_ref, s_gate_h, s_up_h, s_down_h, e_gate_h, e_up_h, e_down_h,
    x_out, hid_out, teacher_out, delta_all, gg_out, ug_out,
    block, mix, gate_out, up_out, ret_ref, delta,
    buf, s_gate, s_up, s_down, e_gate, e_up, e_down, w_sem, x_sem, picked, p_ref, v_acc, v_ref, v_s, v_r, *rest,
):
    w, d = lax.axis_index("wide"), lax.axis_index("dp")
    me = place_of(w)
    weights = ((s_gate_h, s_gate), (s_up_h, s_up), (s_down_h, s_down), (e_gate_h, e_gate), (e_up_h, e_up), (e_down_h, e_down))
    loads = [pltpu.make_async_copy(src, dst, w_sem.at[i]) for i, (src, dst) in enumerate(weights)]
    for c in loads:
        c.start()
    barrier = pltpu.get_barrier_semaphore()

    def hello(off, carry):
        pl.semaphore_signal(barrier, inc=1, device_id={"wide": lax.rem(w + off, NWIDE)}, device_id_type=MESH)
        return carry

    lax.fori_loop(1, NWIDE, hello, 0)
    for peer in dp_peers(d):
        pl.semaphore_signal(barrier, inc=1, device_id=peer, device_id_type=MESH)
    block[:, :cols] = layer_in[...]
    block[:, cols:], mix[...] = routes(ids_ref[...], scores_ref[...], slots)
    pl.semaphore_wait(barrier, NWIDE + 2)

    refs = iter(rest)
    g = Gather(buf, list(itertools.islice(refs, len(Gather.sems))), me)
    st = Direct(list(itertools.islice(refs, 7)), d)
    ex = Exchange(list(itertools.islice(refs, 15)), d)
    red = Reduce(p_ref, list(itertools.islice(refs, 22)), g)
    back = Gather(delta_all, list(itertools.islice(refs, len(Gather.sems))), me)
    hg = Direct(list(itertools.islice(refs, 7)), d)
    unit = s_gate.shape[0] // 4
    tok = NY * NX * rows_per
    tiles = e_gate.shape[0] // E_TILE
    batch = slots // BATCHES
    quarter = batch // 4
    per_chunk = slots // NZ

    def lanes(k):
        return pl.ds(pl.multiple_of(g.zc[k] * tok, tok), tok)

    def student_a(k):
        g.done(k)
        xk = buf[g.zc[k], :, :, :, :cols].reshape(tok, cols)
        for i, weight in enumerate((s_gate, s_up)):
            part = mm(weight[...], xk, ((1,), (1,)))
            for q in range(4):
                st.parts[k, q, i] = part[q * unit : (q + 1) * unit]
        st.send(k)

    def student_c(k):
        both = st.total(k)
        gate, up = both[0], both[1]
        gate_out[:, lanes(k)] = gate
        up_out[:, lanes(k)] = up
        st.out[k, d] = (gate * jax.nn.sigmoid(gate) * up).astype(BF)
        st.share(k)

    def student_e(k):
        st.done(k)
        hid = st.out[k].reshape(4 * unit, tok)
        hid_out[:, lanes(k)] = hid
        p_ref[k] = mm(hid, s_down[...], ((0,), (0,))).astype(BF).reshape(NY, NX, rows_per, cols)
        red.begin(k)

    def pick(k):
        lane = lax.broadcasted_iota(jnp.int32, (16, 128), 1)
        mine = jnp.where(lane == w, 1.0, 0.0).astype(BF)
        code = mm(mine, buf[g.zc[k], :, :, :, cols:].reshape(tok, 128), ((1,), (1,)))[:1]
        at = 4 * lax.div(lax.broadcasted_iota(jnp.int32, (1, tok), 1), rows_per)
        want = lax.broadcasted_iota(jnp.int32, (per_chunk, tok), 0).astype(F32)
        picker = jnp.where(at.astype(F32) + code == want, 1.0, 0.0).astype(BF)
        xk = buf[g.zc[k], :, :, :, :cols].reshape(tok, cols)
        picked[per_chunk * k : per_chunk * (k + 1)] = mm(picker, xk, ((1,), (0,))).astype(BF)

    def expert_a(n):
        if n == 0:
            loads[3].wait()
            loads[4].wait()
        b, i = n // tiles, n % tiles
        for j, weight in enumerate((e_gate, e_up)):
            part = mm(picked[b * batch : (b + 1) * batch], weight[i * E_TILE : (i + 1) * E_TILE], ((1,), (1,)))
            for q in range(4):
                ex.parts[n, q % 2, q // 2, j] = part[q * quarter : (q + 1) * quarter]
        ex.to_mate(n)

    def expert_c(n):
        both = ex.total(n)
        gate, up = both[0], both[1]
        ex.out[n, d] = (gate * jax.nn.sigmoid(gate) * up).astype(BF)
        ex.share(n)

    def expert_e(n):
        if n == 0:
            loads[5].wait()
        b, i = n // tiles, n % tiles
        ex.done(n)
        more = mm(ex.out[n].reshape(batch, E_TILE), e_down[i * E_TILE : (i + 1) * E_TILE], ((1,), (0,)))
        if 0 < i < tiles - 1:
            v_acc[...] += more
        elif i == 0:
            v_acc[...] = more
        else:
            blocks = NWIDE // BATCHES
            v_ref[b * blocks : (b + 1) * blocks] = (v_acc[...] + more).reshape((blocks,) + v_ref.shape[1:]).astype(BF)
            for k in range(b * NZ // BATCHES, (b + 1) * NZ // BATCHES):
                lax.fori_loop(0 if k else 1, NY * NX, functools.partial(send_values, k), 0)

    yh, z, x = me

    def values_copy(k, j):
        to_y, to_x = lax.rem(yh + lax.div(j, NX), NY), lax.rem(x + lax.rem(j, NX), NX)
        at = k * NY * NX + j
        there = wide_of(to_y, g.zc[k], to_x)
        return rcopy(v_ref.at[k * NY * NX + to_y * NX + to_x], ret_ref.at[w], v_s.at[at], v_r.at[at], wide=there)

    def send_values(k, j, carry):
        values_copy(k, j).start()
        return carry

    def wait_values(k, j, carry):
        from_y, from_x = lax.rem(yh + NY - lax.div(j, NX), NY), lax.rem(x + NX - lax.rem(j, NX), NX)
        came = ret_ref.at[wide_of(from_y, lax.rem(z + NEAR_FIRST[k], NZ), from_x)]
        at = k * NY * NX + j
        rcopy(came, came, v_s.at[at], v_r.at[at], wide=g.to_right).wait_recv()
        values_copy(k, j).wait_send()
        return carry

    stages = [(g.spread, 0, NZ), (g.forward, 1, NZ), (student_a, 2, NZ), (student_c, 3, NZ), (student_e, 4, NZ)]
    stages += [(pick, 2, NZ), (red.merge, 5, NZ), (red.total, 6, NZ)]
    half = NZ // BATCHES
    experts = [(expert_a, 0), (ex.to_across, 1), (expert_c, 2), (ex.pass_on, 3), (expert_e, 4)]
    when = [half + 2 + i + b * half for b in range(BATCHES) for i in range(tiles)]
    g.begin(block)
    for c in loads[:3]:
        c.wait()
    for t in range(when[-1] + 5):
        if t == NZ + 2:
            pltpu.make_async_copy(buf.at[:, :, :, :, pl.ds(0, cols)], x_out, x_sem).start()
        for run, lag, count in stages:
            if 0 <= t - lag < count:
                run(t - lag)
        for run, lag in experts:
            if t - lag in when:
                run(when.index(t - lag))
    ret_ref[w] = v_ref[yh * NX + x]
    student_out = red.finish()
    for k in range(NZ):
        lax.fori_loop(0 if k else 1, NY * NX, functools.partial(wait_values, k), 0)
    terms = mm(mix[...], ret_ref[...].reshape(slots, cols), ((1,), (0,)))
    teacher = terms[:rows_per] + terms[rows_per : 2 * rows_per] + terms[2 * rows_per :]
    teacher_out[...] = teacher
    delta[...] = ((student_out - teacher) * (1.0 / math.sqrt(tok * NZ))).astype(BF)

    def part(k):
        back.done(k)
        term = mm(s_down[...], delta_all[back.zc[k]].reshape(tok, cols), ((1,), (1,)))
        for q in range(4):
            hg.parts[k, q] = term[q * unit : (q + 1) * unit]
        hg.send(k)

    def grads(k):
        grad = hg.total(k)
        gate, up = gate_out[:, lanes(k)], up_out[:, lanes(k)]
        s = jax.nn.sigmoid(gate)
        hg.out[k, d, 0] = (grad * up * s * (1.0 + gate * (1.0 - s))).astype(BF)
        hg.out[k, d, 1] = (grad * (gate * s)).astype(BF)
        hg.share(k)

    def store(k):
        hg.done(k)
        for q in range(4):
            gg_out[q * unit : (q + 1) * unit, lanes(k)] = hg.out[k, q, 0]
            ug_out[q * unit : (q + 1) * unit, lanes(k)] = hg.out[k, q, 1]

    back.begin(delta)
    for t in range(NZ + 4):
        for run, lag in ((back.spread, 0), (back.forward, 1), (part, 2), (grads, 3), (store, 4)):
            if 0 <= t - lag < NZ:
                run(t - lag)
    pltpu.make_async_copy(buf.at[:, :, :, :, pl.ds(0, cols)], x_out, x_sem).wait()
    for group in (g, st, ex, back, hg):
        group.end()


VM = pl.BlockSpec(memory_space=pltpu.VMEM)
ANY = pl.BlockSpec(memory_space=pl.ANY)
HBM = pl.BlockSpec(memory_space=pltpu.HBM)


def params(number):
    return pltpu.CompilerParams(collective_id=number, has_side_effects=True, vmem_limit_bytes=50 << 20)


def step(layer_in, ids, scores, s_gate, s_up, s_down, e_gate, e_up, e_down, slots):
    rows, cols = layer_in.shape
    full = cols + 128
    hid = s_gate.shape[0]
    e_hid = e_gate.shape[0]
    unit, tok, tiles, quarter = hid // 4, NY * NX * rows, e_hid // E_TILE, slots // 4 // BATCHES
    tokens = tok * NZ
    values = (NWIDE, slots // NWIDE, cols)
    return pl.pallas_call(
        functools.partial(step_kernel, cols, rows, slots),
        out_shape=(
            jax.ShapeDtypeStruct((NZ, NY, NX, rows, cols), BF),
            jax.ShapeDtypeStruct((hid, tokens), BF),
            jax.ShapeDtypeStruct((rows, cols), F32),
            jax.ShapeDtypeStruct((NZ, NY, NX, rows, cols), BF),
            jax.ShapeDtypeStruct((hid, tokens), BF),
            jax.ShapeDtypeStruct((hid, tokens), BF),
        ),
        in_specs=[VM] * 3 + [HBM] * 6,
        out_specs=(ANY, VM, VM, VM, VM, VM),
        scratch_shapes=[
            pltpu.VMEM((rows, full), BF),
            pltpu.VMEM((3 * rows, slots), BF),
            pltpu.VMEM((unit, tokens), F32),
            pltpu.VMEM((unit, tokens), F32),
            pltpu.VMEM(values, BF),
            pltpu.VMEM((rows, cols), BF),
            pltpu.VMEM((NZ, NY, NX, rows, full), BF),
        ]
        + [pltpu.VMEM((hid, cols), BF)] * 3
        + [pltpu.VMEM((e_hid, cols), BF)] * 3
        + [
            DMA((6,)),
            DMA(()),
            pltpu.VMEM((slots, cols), BF),
            pltpu.VMEM((NZ, NY, NX, rows, cols), BF),
            pltpu.VMEM((slots // BATCHES, cols), F32),
            pltpu.VMEM(values, BF),
            DMA((NWIDE,)),
            DMA((NWIDE,)),
        ]
        + Gather.sems
        + Direct.scratch(NZ, (2, unit, tok), (unit, tok))
        + Exchange.scratch(tiles * BATCHES, (2, quarter, E_TILE), (quarter, E_TILE), BF)
        + Reduce.scratch(rows, cols)
        + Gather.sems
        + Direct.scratch(NZ, (unit, tok), (2, unit, tok)),
        compiler_params=params(0),
        name="step",
    )(layer_in, ids, scores, s_gate, s_up, s_down, e_gate, e_up, e_down)


def dot(a, b, out=BF):
    return mm(a, b, ((1,), (0,))).astype(out)


def shards(
    layer_in,
    route_ids,
    route_scores,
    expert_gate,
    expert_up,
    expert_down,
    student_gate,
    student_up,
    student_down,
):
    columns = layer_in.shape[1]
    gathered, hidden, teacher_sum, delta_all, gg, ug = step(
        layer_in,
        route_ids,
        route_scores,
        student_gate,
        student_up,
        student_down,
        expert_gate[0],
        expert_up[0],
        expert_down[0],
        4 * lax.axis_size("wide"),
    )
    gathered = gathered.reshape(-1, columns)
    grad_down = dot(hidden, delta_all.reshape(-1, columns))
    grad_gate = dot(gg, gathered)
    grad_up = dot(ug, gathered)
    return (teacher_sum.astype(BF), grad_gate, grad_up, grad_down)


def solution(mesh):
    in_specs = (
        P("wide", "dp"),
        P("wide", None),
        P("wide", None),
        P("wide", None, "dp"),
        P("wide", None, "dp"),
        P("wide", None, "dp"),
        P("wide", "dp"),
        P("wide", "dp"),
        P("wide", "dp"),
    )
    out_specs = (P("wide", "dp"), P("wide", "dp"), P("wide", "dp"), P("wide", "dp"))
    return jax.shard_map(shards, mesh=mesh, in_specs=in_specs, out_specs=out_specs, check_vma=False)
```
